32 devices in a mesh: gx: 4 (over z), gy: 8 (over y, x, core).
Axes of the slice: x: 2, y: 2, z: 4, core: 2. Of those that a mesh axis runs over, the one named last changes fastest.
Arguments:
- coeffs: bfloat16 [8, 64, 256, 128], P('gx', 'gy'), may hold values from -0.25 to 0.25
- permit: float32 [8, 64, 256], P('gx', 'gy'), may hold values from 0.25 to 4
- shift_diag: float32 [8, 64, 128], P('gx', 'gy'), may hold values from 0.5 to 4
- codes: int32 [8, 64, 6], P('gx', 'gy'), may hold values from 0 to 8
- counts: int32 [8, 64], P('gx', 'gy'), may hold values from 1 to 6
- weights: float32 [8, 64, 6], P('gx', 'gy'), may hold values from 0.5 to 1.5
- vectors: bfloat16 [8, 64, 128, 128], P('gx', 'gy'), may hold values from -6 to 6
Outputs:
- factor: bfloat16 [8, 64, 128, 128], P('gx', 'gy')
- applied: bfloat16 [8, 64, 128, 128], P('gx', 'gy')
The draws below stay inside these ranges and needn't reach their ends.
Inputs may be any that keep to these rules, and one draw needn't show every extreme that they name: codes name one of the 3 x 3 blocks around a block, as in the reference program.
All inputs are finite; a program needn't handle non-finite values.
Results may differ from the reference program's by a relative error of at most 0.0051.
Values may be sent and summed in bfloat16 or wider, within the bound.
A program may use at most 64 MiB of HBM per device.

```python
import math
import jax
import jax.numpy as jnp
from jax import lax

B = 128
R = 256
NV = 128
PAT = 6
BX = 8
BY = 64


def draw_coeffs(key, part):
    key_cols = jax.random.fold_in(key, 11)
    key_rows = jax.random.fold_in(key, 23)
    column_noise = jax.random.normal(key_cols, (BX, BY, R, B + 1), jnp.float32)
    row_common = jax.random.normal(key_rows, (BX, BY, R, 1), jnp.float32)
    mixed = column_noise[:, :, :, 1:] + 0.9 * column_noise[:, :, :, :-1] + 1.5 * row_common
    values = mixed * jnp.float32(0.031)
    values = jnp.clip(values, -0.25, 0.25)
    return values.astype(jnp.bfloat16)


def touch_ends(values, key, low, largest):
    shape = values.shape
    place = [jax.random.randint(jax.random.fold_in(key, axis), (), 0, shape[axis]) for axis in range(len(shape))]
    values = values.at[tuple(place)].set(low)
    longest = shape.index(max(shape))
    place[longest] = (place[longest] + 1) % shape[longest]
    return values.at[tuple(place)].set(largest)


def steps_of(rng, dims, cuts, low, high):
    def one(dim, blocks):
        heights = jax.random.uniform(jax.random.fold_in(jax.random.fold_in(rng, 6), dim), (blocks,), jnp.float32, low / len(cuts), high / len(cuts))
        return jnp.repeat(jnp.exp(heights), dims[dim] // blocks).reshape((-1,) + (1,) * (len(dims) - dim - 1))

    gain = one(*cuts[0])
    for cut in cuts[1:]:
        gain = gain * one(*cut)
    return gain


def noise(own_key, shape, spread, reach, cuts=(), kind=jnp.bfloat16):
    drawn = jax.random.normal(own_key, shape, jnp.float32) * spread
    if len(cuts) > 0:
        drawn = steps_of(own_key, shape, cuts, -0.22, 0.18) * drawn
    return jnp.clip(drawn, min=-reach, max=reach).astype(kind)


def setup_inputs(seed: int = 0) -> dict:
    keys = jax.random.split(jax.random.key(seed), 8)
    coeffs = draw_coeffs(jax.random.fold_in(keys[7], 71), 0)
    permit = jnp.clip(jnp.exp(math.log(4.0) - 2.7725887 * jax.random.uniform(keys[1], (BX, BY, R), jnp.float32) ** steps_of(keys[1], (BX, BY, R), ((0, 4), (1, 8)), -0.2, 0.2)), 0.25, 4.0)
    shift_diag = jnp.clip(jnp.exp(math.log(4.0) - 2.0794415 * jax.random.uniform(keys[2], (BX, BY, B), jnp.float32) ** steps_of(keys[2], (BX, BY, B), ((0, 4), (1, 8)), -0.2, 0.2)), 0.5, 4.0)
    codes = touch_ends(jax.random.randint(keys[3], (BX, BY, PAT), 0, 9), jax.random.fold_in(keys[3], 1), 0, 8).astype(jnp.int32)
    counts = touch_ends(jax.random.randint(keys[4], (BX, BY), 1, PAT + 1), jax.random.fold_in(keys[4], 1), 1, PAT).astype(jnp.int32)
    weights = jnp.clip(0.5 + 1.0 * jax.random.uniform(keys[5], (BX, BY, PAT), jnp.float32) ** steps_of(keys[5], (BX, BY, PAT), ((0, 4), (1, 8)), -0.2, 0.2), 0.5, 1.5)
    vectors = noise(keys[6], (BX, BY, B, NV), 1.0, 6.0, ((0, 4), (1, 8)))
    return dict(coeffs=coeffs, permit=permit, shift_diag=shift_diag, codes=codes, counts=counts, weights=weights, vectors=vectors)


def reference(coeffs, permit, shift_diag, codes, counts, weights, vectors):
    padded = jnp.pad(coeffs, ((1, 1), (1, 1), (0, 0), (0, 0)))
    columns = jnp.arange(BY)

    def block_row(row_at):
        window = lax.dynamic_slice_in_dim(padded, row_at, 3, 0)
        permit_row = permit[row_at]
        code_row = codes[row_at]
        count_row = counts[row_at]
        gram = jnp.zeros((BY, B, B), jnp.float32)
        for slot_num in range(PAT):
            slot_code = code_row[:, slot_num]
            neighbour = window[slot_code // 3, columns + slot_code % 3]
            scaled = (permit_row[:, :, None] * neighbour.astype(jnp.float32)).astype(jnp.bfloat16)
            product = jnp.einsum('yrk,yrl->ykl', scaled.astype(jnp.float32), neighbour.astype(jnp.float32))
            gram = gram + jnp.where((slot_num < count_row)[:, None, None], product, jnp.float32(0.0))
        system = gram + shift_diag[row_at][:, :, None] * jnp.eye(B, dtype=jnp.float32)
        cholesky_factor = jnp.linalg.cholesky(system)
        identity = jnp.broadcast_to(jnp.eye(B, dtype=system.dtype), system.shape)
        inverse = lax.linalg.triangular_solve(cholesky_factor, identity, left_side=True, lower=True)
        factor_row = inverse.astype(jnp.bfloat16)
        images = jnp.einsum('ykl,ykv->ylv', factor_row.astype(jnp.float32), vectors[row_at].astype(jnp.float32))
        return (factor_row, images)
    factor, images = lax.map(block_row, jnp.arange(BX))
    active = jnp.arange(PAT)[None, None, :] < counts[:, :, None]
    gathered_sum = jnp.zeros((BX + 2, BY + 2, B, NV), jnp.float32)
    for offset in range(9):
        weight_sum = jnp.sum(jnp.where(active & (codes == offset), weights, jnp.float32(0.0)), axis=-1)
        gathered_sum = gathered_sum.at[offset // 3:offset // 3 + BX, offset % 3:offset % 3 + BY].add(weight_sum[:, :, None, None] * images)
    applied = gathered_sum[1:-1, 1:-1].astype(jnp.bfloat16)
    return (factor, applied)
```

```python
import functools

import jax
import jax.numpy as jnp
from jax import lax
from jax.experimental import pallas as pl
from jax.experimental.pallas import tpu as pltpu
from jax.sharding import PartitionSpec as P

MESH = pl.DeviceIdType.MESH
DIRS = ((1, 0), (-1, 0), (0, 1), (0, -1), (1, 1), (1, -1), (-1, 1), (-1, -1))


def neighbours():
    sizes = (lax.axis_size("gx"), lax.axis_size("gy"))
    me = (lax.axis_index("gx"), lax.axis_index("gy"))

    def there(d):
        return (me[0] + d[0], me[1] + d[1])

    def exists(d):
        ok = None
        for size, at, step in zip(sizes, me, d):
            if step == 0:
                continue
            test = (at + 1 < size) if step > 0 else (at > 0)
            ok = test if ok is None else jnp.logical_and(ok, test)
        return ok

    return there, exists


def exchange(sends, lands, send_sem, recv_sem, before=None):
    there, exists = neighbours()
    barrier = pltpu.get_barrier_semaphore()
    for d in DIRS:
        @pl.when(exists(d))
        def _(d=d):
            pl.semaphore_signal(barrier, inc=1, device_id=there(d), device_id_type=MESH)
    near = [exists(d).astype(jnp.int32) for d in DIRS[:4]]
    pl.semaphore_wait(barrier, (near[0] + near[1] + 1) * (near[2] + near[3] + 1) - 1)

    def copy(k, d):
        return pltpu.make_async_remote_copy(
            src_ref=sends[k], dst_ref=lands[k], send_sem=send_sem.at[k], recv_sem=recv_sem.at[k],
            device_id=there(d), device_id_type=MESH)

    for k, d in enumerate(DIRS):
        @pl.when(exists(d))
        def _(k=k, d=d):
            copy(k, d).start()

    def finish():
        for k, d in enumerate(DIRS):
            @pl.when(exists((-d[0], -d[1])))
            def _(k=k, d=d):
                copy(k, d).wait_recv()
        for k, d in enumerate(DIRS):
            @pl.when(exists(d))
            def _(k=k, d=d):
                copy(k, d).wait_send()

    return finish


def halo_kernel(c_ref, hx_ref, hy_ref, hc_ref, send_sem, recv_sem):
    bx, by = c_ref.shape[0], c_ref.shape[1]
    row = {1: bx - 1, -1: 0}
    col = {1: by - 1, -1: 0}
    sends = [c_ref.at[bx - 1], c_ref.at[0], c_ref.at[:, by - 1], c_ref.at[:, 0]]
    lands = [hx_ref.at[0], hx_ref.at[1], hy_ref.at[0], hy_ref.at[1]]
    for k, d in enumerate(DIRS[4:]):
        sends.append(c_ref.at[row[d[0]], col[d[1]]])
        lands.append(hc_ref.at[k])
    exchange(sends, lands, send_sem, recv_sem)()


def factor_kernel(c_ref, hx_ref, hy_ref, hc_ref, permit_ref, shift_ref, codes_ref, counts_ref, weights_ref,
                  v_ref, fac_ref, loc_ref, px_ref, py_ref, pc_ref, cs, ts, gs, ss, sem):
    bx, by, coupling, order = c_ref.shape
    slots = codes_ref.shape[2]
    blocks = bx * by
    wide = by + 2
    nx, ny = lax.axis_size("gx"), lax.axis_size("gy")
    gx, gy = lax.axis_index("gx"), lax.axis_index("gy")
    moves = []
    for x in range(bx):
        moves.append((c_ref.at[x], cs.at[pl.ds((x + 1) * wide + 1, by)]))
        moves.append((hy_ref.at[0, x], cs.at[(x + 1) * wide]))
        moves.append((hy_ref.at[1, x], cs.at[(x + 1) * wide + by + 1]))
    moves.append((hx_ref.at[0], cs.at[pl.ds(1, by)]))
    moves.append((hx_ref.at[1], cs.at[pl.ds((bx + 1) * wide + 1, by)]))
    moves.append((hc_ref.at[0], cs.at[0]))
    moves.append((hc_ref.at[1], cs.at[by + 1]))
    moves.append((hc_ref.at[2], cs.at[(bx + 1) * wide]))
    moves.append((hc_ref.at[3], cs.at[(bx + 1) * wide + by + 1]))
    copies = [pltpu.make_async_copy(a, b, sem.at[k]) for k, (a, b) in enumerate(moves)]
    for copy in copies:
        copy.start()

    @pl.loop(0, (bx + 2) * wide)
    def _(n):
        ss[n] = jnp.zeros(ss.shape[1:], ss.dtype)

    for copy in copies:
        copy.wait()

    @pl.loop(0, (bx + 2) * wide)
    def _(n):
        ts[n] = cs[n].T

    def slot_at(x, y, s):
        code = codes_ref[x, y, s]
        ax, ay = code // 3, code % 3
        whole_x, whole_y = gx * bx + x + ax - 1, gy * by + y + ay - 1
        ok = (s < counts_ref[x, y]) & (whole_x >= 0) & (whole_x < nx * bx) & (whole_y >= 0) & (whole_y < ny * by)
        return jnp.where(ok, (x + ax) * wide + y + ay, (x + 1) * wide + y + 1), ok

    rows = lax.broadcasted_iota(jnp.int32, (order, order), 0)
    lanes = lax.broadcasted_iota(jnp.int32, (order, order), 1)

    @pl.loop(0, blocks)
    def _(i):
        x, y = i // by, i % by
        p = permit_ref[x, pl.ds(y, 1), :]
        acc = jnp.zeros((order, order), jnp.float32)
        for s in range(slots):
            n, ok = slot_at(x, y, s)
            scaled = (ts[n].astype(jnp.float32) * jnp.where(ok, p, 0.0)).astype(jnp.bfloat16)
            acc = acc + jnp.dot(scaled, cs[n], preferred_element_type=jnp.float32)
        gs[i] = 0.5 * (acc + acc.T) + jnp.where(rows == lanes, shift_ref[x, pl.ds(y, 1), :], 0.0)

    parts = 4
    step = order // parts
    for part in range(parts):
        low = part * step
        height = order - low
        row_here = lax.broadcasted_iota(jnp.int32, (height, order), 0) + low
        lane_row = lax.broadcasted_iota(jnp.int32, (1, order), 1)

        @pl.loop(low, low + step)
        def _(k):
            below = row_here > k
            pick = jnp.full((height, order), k, jnp.int32)
            for b in range(blocks):
                m = gs[b, low:, :]
                r = gs[b, pl.ds(k, 1), :]
                d = jnp.sum(jnp.where(lane_row == k, r, 0.0), axis=1, keepdims=True)
                r = (r + jnp.where(lane_row == k, 1.0, 0.0)) / d
                f = jnp.where(below, jnp.take_along_axis(m, pick, axis=1), 0.0)
                gs[b, low:, :] = m - f * r

    @pl.loop(0, blocks)
    def _(i):
        x, y = i // by, i % by
        m = gs[i]
        d = jnp.sum(jnp.where(rows == lanes, m, 0.0), axis=1, keepdims=True)
        inverse = jnp.where(rows > lanes, m, jnp.where(rows == lanes, 1.0, 0.0)) * lax.rsqrt(d)
        factor = inverse.astype(jnp.bfloat16)
        fac_ref[x, y] = factor
        image = lax.dot_general(factor, v_ref[x, y], (((0,), (0,)), ((), ())), preferred_element_type=jnp.float32)
        for s in range(slots):
            n, ok = slot_at(x, y, s)
            w = jnp.where(ok, weights_ref[x, y, s], 0.0)
            ss[n] = ss[n] + w * image

    for x in range(bx):
        for y in range(by):
            loc_ref[x, y] = ss[(x + 1) * wide + y + 1]
        py_ref[1, x] = ss[(x + 1) * wide].astype(jnp.bfloat16)
        py_ref[0, x] = ss[(x + 1) * wide + by + 1].astype(jnp.bfloat16)
    for y in range(by):
        px_ref[1, y] = ss[y + 1].astype(jnp.bfloat16)
        px_ref[0, y] = ss[(bx + 1) * wide + y + 1].astype(jnp.bfloat16)
    pc_ref[0] = ss[(bx + 1) * wide + by + 1].astype(jnp.bfloat16)
    pc_ref[1] = ss[(bx + 1) * wide].astype(jnp.bfloat16)
    pc_ref[2] = ss[by + 1].astype(jnp.bfloat16)
    pc_ref[3] = ss[0].astype(jnp.bfloat16)


def sum_kernel(loc_ref, px_ref, py_ref, pc_ref, out_ref, rx, ry, rc, send_sem, recv_sem):
    bx, by = loc_ref.shape[0], loc_ref.shape[1]
    _, exists = neighbours()
    sends = [px_ref.at[0], px_ref.at[1], py_ref.at[0], py_ref.at[1]] + [pc_ref.at[k] for k in range(4)]
    lands = [rx.at[0], rx.at[1], ry.at[0], ry.at[1]] + [rc.at[k] for k in range(4)]
    for k, d in enumerate(DIRS):
        @pl.when(jnp.logical_not(exists((-d[0], -d[1]))))
        def _(k=k):
            lands[k][...] = jnp.zeros(lands[k].shape, lands[k].dtype)
    exchange(sends, lands, send_sem, recv_sem)()
    corner = {(0, 0): 0, (0, by - 1): 1, (bx - 1, 0): 2, (bx - 1, by - 1): 3}
    for x in range(bx):
        for y in range(by):
            total = loc_ref[x, y]
            for at, edge, k in ((x, 0, 0), (x, bx - 1, 1)):
                if at == edge:
                    total = total + rx[k, y].astype(jnp.float32)
            for at, edge, k in ((y, 0, 0), (y, by - 1, 1)):
                if at == edge:
                    total = total + ry[k, x].astype(jnp.float32)
            for place, k in (((0, 0), 0), ((0, by - 1), 1), ((bx - 1, 0), 2), ((bx - 1, by - 1), 3)):
                if (x, y) == place:
                    total = total + rc[k].astype(jnp.float32)
            out_ref[x, y] = total.astype(out_ref.dtype)


def local(coeffs, permit, shift_diag, codes, counts, weights, vectors):
    bx, by, coupling, order = coeffs.shape
    nv = vectors.shape[3]
    bf16, f32 = jnp.bfloat16, jnp.float32
    anyspace = pl.BlockSpec(memory_space=pl.ANY)
    vmem = pl.BlockSpec(memory_space=pltpu.VMEM)
    smem = pl.BlockSpec(memory_space=pltpu.SMEM)
    halo = pl.pallas_call(
        halo_kernel,
        out_shape=(
            jax.ShapeDtypeStruct((2, by, coupling, order), bf16),
            jax.ShapeDtypeStruct((2, bx, coupling, order), bf16),
            jax.ShapeDtypeStruct((4, coupling, order), bf16),
        ),
        in_specs=[anyspace],
        out_specs=(anyspace,) * 3,
        scratch_shapes=[pltpu.SemaphoreType.DMA((8,)), pltpu.SemaphoreType.DMA((8,))],
        compiler_params=pltpu.CompilerParams(collective_id=0, has_side_effects=True),
        name="halo",
    )(coeffs)
    padded = (bx + 2) * (by + 2)
    fac, loc, px, py, pc = pl.pallas_call(
        factor_kernel,
        out_shape=(
            jax.ShapeDtypeStruct((bx, by, order, order), bf16),
            jax.ShapeDtypeStruct((bx, by, order, nv), f32),
            jax.ShapeDtypeStruct((2, by, order, nv), bf16),
            jax.ShapeDtypeStruct((2, bx, order, nv), bf16),
            jax.ShapeDtypeStruct((4, order, nv), bf16),
        ),
        in_specs=[anyspace] * 4 + [vmem, vmem, smem, smem, smem, vmem],
        out_specs=(vmem,) * 5,
        scratch_shapes=[
            pltpu.VMEM((padded, coupling, order), bf16),
            pltpu.VMEM((padded, order, coupling), bf16),
            pltpu.VMEM((bx * by, order, order), f32),
            pltpu.VMEM((padded, order, nv), f32),
            pltpu.SemaphoreType.DMA((3 * bx + 6,)),
        ],
        name="factor",
    )(coeffs, *halo, permit, shift_diag, codes, counts, weights, vectors)
    applied = pl.pallas_call(
        sum_kernel,
        out_shape=jax.ShapeDtypeStruct((bx, by, order, nv), bf16),
        in_specs=[vmem, anyspace, anyspace, anyspace],
        out_specs=vmem,
        scratch_shapes=[
            pltpu.VMEM((2, by, order, nv), bf16),
            pltpu.VMEM((2, bx, order, nv), bf16),
            pltpu.VMEM((4, order, nv), bf16),
            pltpu.SemaphoreType.DMA((8,)), pltpu.SemaphoreType.DMA((8,)),
        ],
        compiler_params=pltpu.CompilerParams(collective_id=1, has_side_effects=True),
        name="sums",
    )(loc, px, py, pc)
    return fac, applied


def solution(mesh):
    placed = (
        P("gx", "gy", None, None),
        P("gx", "gy", None),
        P("gx", "gy", None),
        P("gx", "gy", None),
        P("gx", "gy"),
        P("gx", "gy", None),
        P("gx", "gy", None, None),
    )
    return jax.shard_map(
        local,
        mesh=mesh,
        in_specs=placed,
        out_specs=(P("gx", "gy", None, None), P("gx", "gy", None, None)),
        check_vma=False,
    )
```

```python
import functools

import jax
import jax.numpy as jnp
from jax import lax
from jax.experimental import pallas as pl
from jax.experimental.pallas import tpu as pltpu
from jax.sharding import PartitionSpec as P

MESH = pl.DeviceIdType.MESH
BASE = 32
DIRS = ((1, 0), (-1, 0), (0, 1), (0, -1), (1, 1), (1, -1), (-1, 1), (-1, -1))


def neighbours():
    sizes = (lax.axis_size("gx"), lax.axis_size("gy"))
    me = (lax.axis_index("gx"), lax.axis_index("gy"))

    def there(d):
        return (me[0] + d[0], me[1] + d[1])

    def exists(d):
        ok = None
        for size, at, step in zip(sizes, me, d):
            if step == 0:
                continue
            test = (at + 1 < size) if step > 0 else (at > 0)
            ok = test if ok is None else jnp.logical_and(ok, test)
        return ok

    return there, exists


def exchange(sends, lands, send_sem, recv_sem, before=None):
    there, exists = neighbours()
    barrier = pltpu.get_barrier_semaphore()
    for d in DIRS:
        @pl.when(exists(d))
        def _(d=d):
            pl.semaphore_signal(barrier, inc=1, device_id=there(d), device_id_type=MESH)
    near = [exists(d).astype(jnp.int32) for d in DIRS[:4]]
    pl.semaphore_wait(barrier, (near[0] + near[1] + 1) * (near[2] + near[3] + 1) - 1)

    def copy(k, d):
        return pltpu.make_async_remote_copy(
            src_ref=sends[k], dst_ref=lands[k], send_sem=send_sem.at[k], recv_sem=recv_sem.at[k],
            device_id=there(d), device_id_type=MESH)

    for k, d in enumerate(DIRS):
        @pl.when(exists(d))
        def _(k=k, d=d):
            copy(k, d).start()

    def finish():
        for k, d in enumerate(DIRS):
            @pl.when(exists((-d[0], -d[1])))
            def _(k=k, d=d):
                copy(k, d).wait_recv()
        for k, d in enumerate(DIRS):
            @pl.when(exists(d))
            def _(k=k, d=d):
                copy(k, d).wait_send()

    return finish


def halo_kernel(c_ref, hx_ref, hy_ref, hc_ref, send_sem, recv_sem):
    bx, by = c_ref.shape[0], c_ref.shape[1]
    row = {1: bx - 1, -1: 0}
    col = {1: by - 1, -1: 0}
    sends = [c_ref.at[bx - 1], c_ref.at[0], c_ref.at[:, by - 1], c_ref.at[:, 0]]
    lands = [hx_ref.at[0], hx_ref.at[1], hy_ref.at[0], hy_ref.at[1]]
    for k, d in enumerate(DIRS[4:]):
        sends.append(c_ref.at[row[d[0]], col[d[1]]])
        lands.append(hc_ref.at[k])
    exchange(sends, lands, send_sem, recv_sem)()


def factor_kernel(c_ref, hx_ref, hy_ref, hc_ref, permit_ref, shift_ref, codes_ref, counts_ref, weights_ref,
                  v_ref, fac_ref, loc_ref, px_ref, py_ref, pc_ref, cs, ts, gs, ss, sem):
    bx, by, coupling, order = c_ref.shape
    slots = codes_ref.shape[2]
    blocks = bx * by
    wide = by + 2
    nx, ny = lax.axis_size("gx"), lax.axis_size("gy")
    gx, gy = lax.axis_index("gx"), lax.axis_index("gy")
    moves = []
    for x in range(bx):
        moves.append((c_ref.at[x], cs.at[pl.ds((x + 1) * wide + 1, by)]))
        moves.append((hy_ref.at[0, x], cs.at[(x + 1) * wide]))
        moves.append((hy_ref.at[1, x], cs.at[(x + 1) * wide + by + 1]))
    moves.append((hx_ref.at[0], cs.at[pl.ds(1, by)]))
    moves.append((hx_ref.at[1], cs.at[pl.ds((bx + 1) * wide + 1, by)]))
    moves.append((hc_ref.at[0], cs.at[0]))
    moves.append((hc_ref.at[1], cs.at[by + 1]))
    moves.append((hc_ref.at[2], cs.at[(bx + 1) * wide]))
    moves.append((hc_ref.at[3], cs.at[(bx + 1) * wide + by + 1]))
    copies = [pltpu.make_async_copy(a, b, sem.at[k]) for k, (a, b) in enumerate(moves)]
    for copy in copies:
        copy.start()

    @pl.loop(0, (bx + 2) * wide)
    def _(n):
        ss[n] = jnp.zeros(ss.shape[1:], ss.dtype)

    for copy in copies:
        copy.wait()

    @pl.loop(0, (bx + 2) * wide)
    def _(n):
        ts[n] = cs[n].T

    def slot_at(x, y, s):
        code = codes_ref[x, y, s]
        ax, ay = code // 3, code % 3
        whole_x, whole_y = gx * bx + x + ax - 1, gy * by + y + ay - 1
        ok = (s < counts_ref[x, y]) & (whole_x >= 0) & (whole_x < nx * bx) & (whole_y >= 0) & (whole_y < ny * by)
        return jnp.where(ok, (x + ax) * wide + y + ay, (x + 1) * wide + y + 1), ok

    rows = lax.broadcasted_iota(jnp.int32, (order, order), 0)
    lanes = lax.broadcasted_iota(jnp.int32, (order, order), 1)

    @pl.loop(0, blocks)
    def _(i):
        x, y = i // by, i % by
        p = permit_ref[x, pl.ds(y, 1), :]
        acc = jnp.zeros((order, order), jnp.float32)
        for s in range(slots):
            n, ok = slot_at(x, y, s)
            scaled = (ts[n].astype(jnp.float32) * jnp.where(ok, p, 0.0)).astype(jnp.bfloat16)
            acc = acc + jnp.dot(scaled, cs[n], preferred_element_type=jnp.float32)
        gs[i] = 0.5 * (acc + acc.T) + jnp.where(rows == lanes, shift_ref[x, pl.ds(y, 1), :], 0.0)

    per = order // BASE
    seg = lax.broadcasted_iota(jnp.int32, (BASE, order), 1) // BASE
    place = lax.broadcasted_iota(jnp.int32, (BASE, order), 1) % BASE
    row = lax.broadcasted_iota(jnp.int32, (BASE, order), 0)
    for stage in range(per):
        low = stage * BASE
        high = low + BASE
        packs = []
        for g in range(blocks // per):
            pack = None
            for q in range(per):
                piece = gs[g * per + q, low:high, :]
                shift = (q * BASE - low) % order
                piece = pltpu.roll(piece, shift, axis=1) if shift else piece
                pack = piece if pack is None else jnp.where(seg == q, piece, pack)
            packs.append(pack)
        done = [[] for _ in packs]
        scale = [[] for _ in packs]
        for k in range(BASE):
            top = k // 8 * 8
            for g, m in enumerate(packs):
                f = jnp.take_along_axis(m, seg[top:] * BASE + k, axis=1)
                d = f[k - top:k - top + 1]
                r = m[k - top:k - top + 1]
                scale[g].append(lax.rsqrt(d))
                r = (r + jnp.where(place[:1] == k, 1.0, 0.0)) * (1.0 / d)
                m = m - jnp.where(row[top:] > k, f, 0.0) * r
                if k % 8 == 7:
                    done[g].append(m[:8])
                    m = m[8:]
                packs[g] = m
        for g in range(len(packs)):
            m = jnp.concatenate(done[g], axis=0)
            unit = jnp.where(row > place, m, jnp.where(row == place, 1.0, 0.0))
            inv = unit * jnp.concatenate(scale[g], axis=0)
            wide_inv = jnp.concatenate([jnp.where(seg == q, inv, 0.0) for q in range(per)], axis=0)
            panel = []
            for q in range(per):
                here = gs[g * per + q, low:high, :]
                panel.append(jnp.where(seg == stage, jnp.where(row == place, 1.0, 0.0), here))
            panel = jnp.concatenate(panel, axis=0)
            whole = jnp.dot(wide_inv, panel, precision=lax.Precision.HIGHEST, preferred_element_type=jnp.float32)
            for q in range(per):
                at = g * per + q
                part = whole[q * BASE:(q + 1) * BASE]
                gs[at, low:high, :] = jnp.where(seg <= stage, part, 0.0)
                if high < order:
                    h = part.astype(jnp.bfloat16)
                    rest = part - h.astype(jnp.float32)
                    m = rest.astype(jnp.bfloat16)
                    l = (rest - m.astype(jnp.float32)).astype(jnp.bfloat16)
                    update = lax.dot_general(
                        jnp.concatenate([h, h, m, h, l, m], axis=0), jnp.concatenate([h, m, h, l, h, m], axis=0),
                        (((0,), (0,)), ((), ())), preferred_element_type=jnp.float32)
                    below = gs[at, high:, :]
                    below = jnp.where(lanes[high:] // BASE == stage, 0.0, below)
                    gs[at, high:, :] = below - update[high:]

    @pl.loop(0, blocks)
    def _(i):
        x, y = i // by, i % by
        factor = gs[i].astype(jnp.bfloat16)
        fac_ref[x, y] = factor
        image = lax.dot_general(factor, v_ref[x, y], (((0,), (0,)), ((), ())), preferred_element_type=jnp.float32)
        for s in range(slots):
            n, ok = slot_at(x, y, s)
            w = jnp.where(ok, weights_ref[x, y, s], 0.0)
            ss[n] = ss[n] + w * image

    for x in range(bx):
        for y in range(by):
            loc_ref[x, y] = ss[(x + 1) * wide + y + 1]
        py_ref[1, x] = ss[(x + 1) * wide].astype(jnp.bfloat16)
        py_ref[0, x] = ss[(x + 1) * wide + by + 1].astype(jnp.bfloat16)
    for y in range(by):
        px_ref[1, y] = ss[y + 1].astype(jnp.bfloat16)
        px_ref[0, y] = ss[(bx + 1) * wide + y + 1].astype(jnp.bfloat16)
    pc_ref[0] = ss[(bx + 1) * wide + by + 1].astype(jnp.bfloat16)
    pc_ref[1] = ss[(bx + 1) * wide].astype(jnp.bfloat16)
    pc_ref[2] = ss[by + 1].astype(jnp.bfloat16)
    pc_ref[3] = ss[0].astype(jnp.bfloat16)


def sum_kernel(loc_ref, px_ref, py_ref, pc_ref, out_ref, rx, ry, rc, send_sem, recv_sem):
    bx, by = loc_ref.shape[0], loc_ref.shape[1]
    _, exists = neighbours()
    sends = [px_ref.at[0], px_ref.at[1], py_ref.at[0], py_ref.at[1]] + [pc_ref.at[k] for k in range(4)]
    lands = [rx.at[0], rx.at[1], ry.at[0], ry.at[1]] + [rc.at[k] for k in range(4)]
    for k, d in enumerate(DIRS):
        @pl.when(jnp.logical_not(exists((-d[0], -d[1]))))
        def _(k=k):
            lands[k][...] = jnp.zeros(lands[k].shape, lands[k].dtype)
    exchange(sends, lands, send_sem, recv_sem)()
    corner = {(0, 0): 0, (0, by - 1): 1, (bx - 1, 0): 2, (bx - 1, by - 1): 3}
    for x in range(bx):
        for y in range(by):
            total = loc_ref[x, y]
            for at, edge, k in ((x, 0, 0), (x, bx - 1, 1)):
                if at == edge:
                    total = total + rx[k, y].astype(jnp.float32)
            for at, edge, k in ((y, 0, 0), (y, by - 1, 1)):
                if at == edge:
                    total = total + ry[k, x].astype(jnp.float32)
            for place, k in (((0, 0), 0), ((0, by - 1), 1), ((bx - 1, 0), 2), ((bx - 1, by - 1), 3)):
                if (x, y) == place:
                    total = total + rc[k].astype(jnp.float32)
            out_ref[x, y] = total.astype(out_ref.dtype)


def local(coeffs, permit, shift_diag, codes, counts, weights, vectors):
    bx, by, coupling, order = coeffs.shape
    nv = vectors.shape[3]
    bf16, f32 = jnp.bfloat16, jnp.float32
    anyspace = pl.BlockSpec(memory_space=pl.ANY)
    vmem = pl.BlockSpec(memory_space=pltpu.VMEM)
    smem = pl.BlockSpec(memory_space=pltpu.SMEM)
    halo = pl.pallas_call(
        halo_kernel,
        out_shape=(
            jax.ShapeDtypeStruct((2, by, coupling, order), bf16),
            jax.ShapeDtypeStruct((2, bx, coupling, order), bf16),
            jax.ShapeDtypeStruct((4, coupling, order), bf16),
        ),
        in_specs=[anyspace],
        out_specs=(anyspace,) * 3,
        scratch_shapes=[pltpu.SemaphoreType.DMA((8,)), pltpu.SemaphoreType.DMA((8,))],
        compiler_params=pltpu.CompilerParams(collective_id=0, has_side_effects=True),
        name="halo",
    )(coeffs)
    padded = (bx + 2) * (by + 2)
    fac, loc, px, py, pc = pl.pallas_call(
        factor_kernel,
        out_shape=(
            jax.ShapeDtypeStruct((bx, by, order, order), bf16),
            jax.ShapeDtypeStruct((bx, by, order, nv), f32),
            jax.ShapeDtypeStruct((2, by, order, nv), bf16),
            jax.ShapeDtypeStruct((2, bx, order, nv), bf16),
            jax.ShapeDtypeStruct((4, order, nv), bf16),
        ),
        in_specs=[anyspace] * 4 + [vmem, vmem, smem, smem, smem, vmem],
        out_specs=(vmem,) * 5,
        scratch_shapes=[
            pltpu.VMEM((padded, coupling, order), bf16),
            pltpu.VMEM((padded, order, coupling), bf16),
            pltpu.VMEM((bx * by, order, order), f32),
            pltpu.VMEM((padded, order, nv), f32),
            pltpu.SemaphoreType.DMA((3 * bx + 6,)),
        ],
        name="factor",
    )(coeffs, *halo, permit, shift_diag, codes, counts, weights, vectors)
    applied = pl.pallas_call(
        sum_kernel,
        out_shape=jax.ShapeDtypeStruct((bx, by, order, nv), bf16),
        in_specs=[vmem, anyspace, anyspace, anyspace],
        out_specs=vmem,
        scratch_shapes=[
            pltpu.VMEM((2, by, order, nv), bf16),
            pltpu.VMEM((2, bx, order, nv), bf16),
            pltpu.VMEM((4, order, nv), bf16),
            pltpu.SemaphoreType.DMA((8,)), pltpu.SemaphoreType.DMA((8,)),
        ],
        compiler_params=pltpu.CompilerParams(collective_id=1, has_side_effects=True),
        name="sums",
    )(loc, px, py, pc)
    return fac, applied


def solution(mesh):
    placed = (
        P("gx", "gy", None, None),
        P("gx", "gy", None),
        P("gx", "gy", None),
        P("gx", "gy", None),
        P("gx", "gy"),
        P("gx", "gy", None),
        P("gx", "gy", None, None),
    )
    return jax.shard_map(
        local,
        mesh=mesh,
        in_specs=placed,
        out_specs=(P("gx", "gy", None, None), P("gx", "gy", None, None)),
        check_vma=False,
    )
```

```python
import functools

import jax
import jax.numpy as jnp
from jax import lax
from jax.experimental import pallas as pl
from jax.experimental.pallas import tpu as pltpu
from jax.sharding import PartitionSpec as P

MESH = pl.DeviceIdType.MESH
BASE = 32
DIRS = ((1, 0), (-1, 0), (0, 1), (0, -1), (1, 1), (1, -1), (-1, 1), (-1, -1))


def neighbours():
    sizes = (lax.axis_size("gx"), lax.axis_size("gy"))
    me = (lax.axis_index("gx"), lax.axis_index("gy"))

    def there(d):
        return (me[0] + d[0], me[1] + d[1])

    def exists(d):
        ok = None
        for size, at, step in zip(sizes, me, d):
            if step == 0:
                continue
            test = (at + 1 < size) if step > 0 else (at > 0)
            ok = test if ok is None else jnp.logical_and(ok, test)
        return ok

    return there, exists


def exchange(sends, lands, send_sem, recv_sem, before=None):
    there, exists = neighbours()
    barrier = pltpu.get_barrier_semaphore()
    for d in DIRS:
        @pl.when(exists(d))
        def _(d=d):
            pl.semaphore_signal(barrier, inc=1, device_id=there(d), device_id_type=MESH)
    near = [exists(d).astype(jnp.int32) for d in DIRS[:4]]
    pl.semaphore_wait(barrier, (near[0] + near[1] + 1) * (near[2] + near[3] + 1) - 1)

    def copy(k, d):
        return pltpu.make_async_remote_copy(
            src_ref=sends[k], dst_ref=lands[k], send_sem=send_sem.at[k], recv_sem=recv_sem.at[k],
            device_id=there(d), device_id_type=MESH)

    for k, d in enumerate(DIRS):
        @pl.when(exists(d))
        def _(k=k, d=d):
            copy(k, d).start()

    def finish():
        for k, d in enumerate(DIRS):
            @pl.when(exists((-d[0], -d[1])))
            def _(k=k, d=d):
                copy(k, d).wait_recv()
        for k, d in enumerate(DIRS):
            @pl.when(exists(d))
            def _(k=k, d=d):
                copy(k, d).wait_send()

    return finish


def gram_kernel(c_ref, permit_ref, shift_ref, codes_ref, counts_ref, gram_ref, cs, ts, own_sem, send_sem, recv_sem):
    bx, by, coupling, order = c_ref.shape
    slots = codes_ref.shape[0]
    wide = by + 2
    there, exists = neighbours()
    row = {1: bx - 1, -1: 0}
    col = {1: by - 1, -1: 0}
    land_row = {1: 0, -1: bx + 1}
    land_col = {1: 0, -1: by + 1}
    gx_dirs, gy_dirs, corners = DIRS[:2], DIRS[2:4], DIRS[4:]
    own = [pltpu.make_async_copy(c_ref.at[x], cs.at[pl.ds((x + 1) * wide + 1, by)], own_sem.at[x]) for x in range(bx)]
    for copy in own:
        copy.start()
    barrier = pltpu.get_barrier_semaphore()
    for d in DIRS:
        @pl.when(exists(d))
        def _(d=d):
            pl.semaphore_signal(barrier, inc=1, device_id=there(d), device_id_type=MESH)
    near = [exists(d).astype(jnp.int32) for d in DIRS[:4]]
    pl.semaphore_wait(barrier, (near[0] + near[1] + 1) * (near[2] + near[3] + 1) - 1)

    def remote(source, target, k, d):
        return pltpu.make_async_remote_copy(
            src_ref=source, dst_ref=cs.at[target], send_sem=send_sem.at[k], recv_sem=recv_sem.at[k],
            device_id=there(d), device_id_type=MESH)

    def gy_copy(j, x):
        d = gy_dirs[j]
        return remote(c_ref.at[x, col[d[1]]], (x + 1) * wide + land_col[d[1]], 4 + j * bx + x, d)

    def corner_copy(j):
        d = corners[j]
        return remote(c_ref.at[row[d[0]], col[d[1]]], land_row[d[0]] * wide + land_col[d[1]], j, d)

    def gx_copy(j, y):
        d = gx_dirs[j]
        return remote(c_ref.at[row[d[0]], y], land_row[d[0]] * wide + y + 1, 4 + 2 * bx + 2 * y + j, d)

    for j, d in enumerate(corners):
        @pl.when(exists(d))
        def _(j=j):
            corner_copy(j).start()
    for j, d in enumerate(gx_dirs):
        @pl.when(exists(d))
        def _(j=j):
            for y in range(by):
                gx_copy(j, y).start()
    for j, d in enumerate(gy_dirs):
        @pl.when(exists(d))
        def _(j=j):
            for x in range(bx):
                gy_copy(j, x).start()

    zero = jnp.zeros((coupling, order), cs.dtype)
    for j, d in enumerate(corners):
        @pl.when(jnp.logical_not(exists((-d[0], -d[1]))))
        def _(d=d):
            cs[land_row[d[0]] * wide + land_col[d[1]]] = zero
    for j, d in enumerate(gx_dirs):
        @pl.when(jnp.logical_not(exists((-d[0], -d[1]))))
        def _(d=d):
            @pl.loop(0, by)
            def _(y):
                cs[land_row[d[0]] * wide + y + 1] = zero
    for j, d in enumerate(gy_dirs):
        @pl.when(jnp.logical_not(exists((-d[0], -d[1]))))
        def _(d=d):
            for x in range(bx):
                cs[(x + 1) * wide + land_col[d[1]]] = zero

    def turn(n):
        ts[n] = cs[n].T

    def terms(x, y, pairs):
        p = permit_ref[x, pl.ds(y, 1), :]
        acc = None
        for ax, ay in pairs:
            n = (x + ax) * wide + y + ay
            times = jnp.int32(0)
            for s in range(slots):
                hit = (codes_ref[s, x, y] == ax * 3 + ay) & (s < counts_ref[x, y])
                times = times + hit.astype(jnp.int32)
            scaled = (ts[n].astype(jnp.float32) * p).astype(jnp.bfloat16)
            term = times.astype(jnp.float32) * jnp.dot(scaled, cs[n], preferred_element_type=jnp.float32)
            acc = term if acc is None else acc + term
        return acc

    inside = {x: [ax for ax in range(3) if 0 <= x + ax - 1 < bx] for x in range(bx)}
    outside = {x: [ax for ax in range(3) if not 0 <= x + ax - 1 < bx] for x in range(bx)}
    for copy in own:
        copy.wait()
    for x in range(bx):
        @pl.loop(0, by)
        def _(y):
            turn((x + 1) * wide + y + 1)
    for x in range(bx):
        @pl.loop(1, by - 1)
        def _(y):
            gram_ref[x, y] = terms(x, y, [(ax, ay) for ax in inside[x] for ay in range(3)])
    for j, d in enumerate(gy_dirs):
        @pl.when(exists((-d[0], -d[1])))
        def _(j=j):
            for x in range(bx):
                gy_copy(j, x).wait_recv()
    for x in range(bx):
        turn((x + 1) * wide)
        turn((x + 1) * wide + by + 1)
    for x in range(bx):
        @pl.loop(0, 2)
        def _(e):
            y = e * (by - 1)
            gram_ref[x, y] = terms(x, y, [(ax, ay) for ax in inside[x] for ay in range(3)])

    same = lax.broadcasted_iota(jnp.int32, (order, order), 0) == lax.broadcasted_iota(jnp.int32, (order, order), 1)

    def finished(x, y, acc):
        gram_ref[x, y] = 0.5 * (acc + acc.T) + jnp.where(same, shift_ref[x, pl.ds(y, 1), :], 0.0)

    for x in range(1, bx - 1):
        @pl.loop(0, by)
        def _(y):
            finished(x, y, gram_ref[x, y])
    for j, d in enumerate(corners):
        @pl.when(exists((-d[0], -d[1])))
        def _(j=j):
            corner_copy(j).wait_recv()
    for r in (0, bx + 1):
        turn(r * wide)
        turn(r * wide + by + 1)

    def arrive(y):
        for j, d in enumerate(gx_dirs):
            @pl.when(exists((-d[0], -d[1])))
            def _(j=j):
                gx_copy(j, y).wait_recv()
        turn(y + 1)
        turn((bx + 1) * wide + y + 1)

    def last(y):
        for x in sorted({0, bx - 1}):
            finished(x, y, gram_ref[x, y] + terms(x, y, [(ax, ay) for ax in outside[x] for ay in range(3)]))

    arrive(0)

    @pl.loop(1, by)
    def _(y):
        arrive(y)
        last(y - 1)

    last(by - 1)
    for j, d in enumerate(corners):
        @pl.when(exists(d))
        def _(j=j):
            corner_copy(j).wait_send()
    for j, d in enumerate(gx_dirs):
        @pl.when(exists(d))
        def _(j=j):
            for y in range(by):
                gx_copy(j, y).wait_send()
    for j, d in enumerate(gy_dirs):
        @pl.when(exists(d))
        def _(j=j):
            for x in range(bx):
                gy_copy(j, x).wait_send()


def factor_kernel(gram_ref, codes_ref, counts_ref, weights_ref, v_ref, fac_ref, loc_ref, px_ref, py_ref, pc_ref, gs, ss):
    bx, by, order = gram_ref.shape[:3]
    slots = codes_ref.shape[0]
    blocks = bx * by
    wide = by + 2
    nx, ny = lax.axis_size("gx"), lax.axis_size("gy")
    gx, gy = lax.axis_index("gx"), lax.axis_index("gy")

    @pl.loop(0, (bx + 2) * wide)
    def _(n):
        ss[n] = jnp.zeros(ss.shape[1:], ss.dtype)

    for i in range(blocks):
        gs[i] = gram_ref[i // by, i % by]

    def slot_at(x, y, s):
        code = codes_ref[s, x, y]
        ax, ay = code // 3, code % 3
        whole_x, whole_y = gx * bx + x + ax - 1, gy * by + y + ay - 1
        ok = (s < counts_ref[x, y]) & (whole_x >= 0) & (whole_x < nx * bx) & (whole_y >= 0) & (whole_y < ny * by)
        return jnp.where(ok, (x + ax) * wide + y + ay, (x + 1) * wide + y + 1), ok

    lanes = lax.broadcasted_iota(jnp.int32, (order, order), 1)
    per = order // BASE
    seg = lax.broadcasted_iota(jnp.int32, (BASE, order), 1) // BASE
    place = lax.broadcasted_iota(jnp.int32, (BASE, order), 1) % BASE
    row = lax.broadcasted_iota(jnp.int32, (BASE, order), 0)
    for stage in range(per):
        low = stage * BASE
        high = low + BASE
        packs = []
        for g in range(blocks // per):
            pack = None
            for q in range(per):
                piece = gs[g * per + q, low:high, :]
                shift = (q * BASE - low) % order
                piece = pltpu.roll(piece, shift, axis=1) if shift else piece
                pack = piece if pack is None else jnp.where(seg == q, piece, pack)
            packs.append(pack)
        done = [[] for _ in packs]
        scale = [[] for _ in packs]
        for k in range(BASE):
            top = k // 8 * 8
            for g, m in enumerate(packs):
                f = jnp.take_along_axis(m, seg[top:] * BASE + k, axis=1)
                d = f[k - top:k - top + 1]
                r = m[k - top:k - top + 1]
                scale[g].append(lax.rsqrt(d))
                r = (r + jnp.where(place[:1] == k, 1.0, 0.0)) * (1.0 / d)
                m = m - jnp.where(row[top:] > k, f, 0.0) * r
                if k % 8 == 7:
                    done[g].append(m[:8])
                    m = m[8:]
                packs[g] = m
        for g in range(len(packs)):
            m = jnp.concatenate(done[g], axis=0)
            unit = jnp.where(row > place, m, jnp.where(row == place, 1.0, 0.0))
            inv = unit * jnp.concatenate(scale[g], axis=0)
            wide_inv = jnp.concatenate([jnp.where(seg == q, inv, 0.0) for q in range(per)], axis=0)
            panel = []
            for q in range(per):
                here = gs[g * per + q, low:high, :]
                panel.append(jnp.where(seg == stage, jnp.where(row == place, 1.0, 0.0), here))
            panel = jnp.concatenate(panel, axis=0)
            whole = jnp.dot(wide_inv, panel, precision=lax.Precision.HIGHEST, preferred_element_type=jnp.float32)
            for q in range(per):
                at = g * per + q
                part = whole[q * BASE:(q + 1) * BASE]
                gs[at, low:high, :] = jnp.where(seg <= stage, part, 0.0)
                if high < order:
                    h = part.astype(jnp.bfloat16)
                    rest = part - h.astype(jnp.float32)
                    m = rest.astype(jnp.bfloat16)
                    l = (rest - m.astype(jnp.float32)).astype(jnp.bfloat16)
                    update = lax.dot_general(
                        jnp.concatenate([h, h, m, h, l, m], axis=0), jnp.concatenate([h, m, h, l, h, m], axis=0),
                        (((0,), (0,)), ((), ())), preferred_element_type=jnp.float32)
                    below = gs[at, high:, :]
                    below = jnp.where(lanes[high:] // BASE == stage, 0.0, below)
                    gs[at, high:, :] = below - update[high:]

    @pl.loop(0, blocks)
    def _(i):
        x, y = i // by, i % by
        factor = gs[i].astype(jnp.bfloat16)
        fac_ref[x, y] = factor
        image = lax.dot_general(factor, v_ref[x, y], (((0,), (0,)), ((), ())), preferred_element_type=jnp.float32)
        for s in range(slots):
            n, ok = slot_at(x, y, s)
            w = jnp.where(ok, weights_ref[s, x, y], 0.0)
            ss[n] = ss[n] + w * image

    for x in range(bx):
        for y in range(by):
            loc_ref[x, y] = ss[(x + 1) * wide + y + 1]
        py_ref[1, x] = ss[(x + 1) * wide].astype(jnp.bfloat16)
        py_ref[0, x] = ss[(x + 1) * wide + by + 1].astype(jnp.bfloat16)
    for y in range(by):
        px_ref[1, y] = ss[y + 1].astype(jnp.bfloat16)
        px_ref[0, y] = ss[(bx + 1) * wide + y + 1].astype(jnp.bfloat16)
    pc_ref[0] = ss[(bx + 1) * wide + by + 1].astype(jnp.bfloat16)
    pc_ref[1] = ss[(bx + 1) * wide].astype(jnp.bfloat16)
    pc_ref[2] = ss[by + 1].astype(jnp.bfloat16)
    pc_ref[3] = ss[0].astype(jnp.bfloat16)


def sum_kernel(loc_ref, px_ref, py_ref, pc_ref, out_ref, rx, ry, rc, send_sem, recv_sem):
    bx, by = loc_ref.shape[0], loc_ref.shape[1]
    _, exists = neighbours()
    sends = [px_ref.at[0], px_ref.at[1], py_ref.at[0], py_ref.at[1]] + [pc_ref.at[k] for k in range(4)]
    lands = [rx.at[0], rx.at[1], ry.at[0], ry.at[1]] + [rc.at[k] for k in range(4)]
    for k, d in enumerate(DIRS):
        @pl.when(jnp.logical_not(exists((-d[0], -d[1]))))
        def _(k=k):
            lands[k][...] = jnp.zeros(lands[k].shape, lands[k].dtype)
    exchange(sends, lands, send_sem, recv_sem)()
    corner = {(0, 0): 0, (0, by - 1): 1, (bx - 1, 0): 2, (bx - 1, by - 1): 3}
    for x in range(bx):
        for y in range(by):
            total = loc_ref[x, y]
            for at, edge, k in ((x, 0, 0), (x, bx - 1, 1)):
                if at == edge:
                    total = total + rx[k, y].astype(jnp.float32)
            for at, edge, k in ((y, 0, 0), (y, by - 1, 1)):
                if at == edge:
                    total = total + ry[k, x].astype(jnp.float32)
            for place, k in (((0, 0), 0), ((0, by - 1), 1), ((bx - 1, 0), 2), ((bx - 1, by - 1), 3)):
                if (x, y) == place:
                    total = total + rc[k].astype(jnp.float32)
            out_ref[x, y] = total.astype(out_ref.dtype)


def local(coeffs, permit, shift_diag, codes, counts, weights, vectors):
    bx, by, coupling, order = coeffs.shape
    nv = vectors.shape[3]
    bf16, f32 = jnp.bfloat16, jnp.float32
    anyspace = pl.BlockSpec(memory_space=pl.ANY)
    vmem = pl.BlockSpec(memory_space=pltpu.VMEM)
    smem = pl.BlockSpec(memory_space=pltpu.SMEM)
    codes, weights = jnp.transpose(codes, (2, 0, 1)), jnp.transpose(weights, (2, 0, 1))
    padded = (bx + 2) * (by + 2)
    copies = 4 + 2 * bx + 2 * by
    gram = pl.pallas_call(
        gram_kernel,
        out_shape=jax.ShapeDtypeStruct((bx, by, order, order), f32),
        in_specs=[anyspace, vmem, vmem, smem, smem],
        out_specs=vmem,
        scratch_shapes=[
            pltpu.VMEM((padded, coupling, order), bf16),
            pltpu.VMEM((padded, order, coupling), bf16),
            pltpu.SemaphoreType.DMA((bx,)),
            pltpu.SemaphoreType.DMA((copies,)), pltpu.SemaphoreType.DMA((copies,)),
        ],
        compiler_params=pltpu.CompilerParams(collective_id=0, has_side_effects=True),
        name="gram",
    )(coeffs, permit, shift_diag, codes, counts)
    fac, loc, px, py, pc = pl.pallas_call(
        factor_kernel,
        out_shape=(
            jax.ShapeDtypeStruct((bx, by, order, order), bf16),
            jax.ShapeDtypeStruct((bx, by, order, nv), f32),
            jax.ShapeDtypeStruct((2, by, order, nv), bf16),
            jax.ShapeDtypeStruct((2, bx, order, nv), bf16),
            jax.ShapeDtypeStruct((4, order, nv), bf16),
        ),
        in_specs=[vmem, smem, smem, smem, vmem],
        out_specs=(vmem,) * 5,
        scratch_shapes=[
            pltpu.VMEM((bx * by, order, order), f32),
            pltpu.VMEM((padded, order, nv), f32),
        ],
        name="factor",
    )(gram, codes, counts, weights, vectors)
    applied = pl.pallas_call(
        sum_kernel,
        out_shape=jax.ShapeDtypeStruct((bx, by, order, nv), bf16),
        in_specs=[vmem, anyspace, anyspace, anyspace],
        out_specs=vmem,
        scratch_shapes=[
            pltpu.VMEM((2, by, order, nv), bf16),
            pltpu.VMEM((2, bx, order, nv), bf16),
            pltpu.VMEM((4, order, nv), bf16),
            pltpu.SemaphoreType.DMA((8,)), pltpu.SemaphoreType.DMA((8,)),
        ],
        compiler_params=pltpu.CompilerParams(collective_id=1, has_side_effects=True),
        name="sums",
    )(loc, px, py, pc)
    return fac, applied


def solution(mesh):
    placed = (
        P("gx", "gy", None, None),
        P("gx", "gy", None),
        P("gx", "gy", None),
        P("gx", "gy", None),
        P("gx", "gy"),
        P("gx", "gy", None),
        P("gx", "gy", None, None),
    )
    return jax.shard_map(
        local,
        mesh=mesh,
        in_specs=placed,
        out_specs=(P("gx", "gy", None, None), P("gx", "gy", None, None)),
        check_vma=False,
    )
```

```python
import functools

import jax
import jax.numpy as jnp
from jax import lax
from jax.experimental import pallas as pl
from jax.experimental.pallas import tpu as pltpu
from jax.sharding import PartitionSpec as P

MESH = pl.DeviceIdType.MESH
BASE = 32
DIRS = ((1, 0), (-1, 0), (0, 1), (0, -1), (1, 1), (1, -1), (-1, 1), (-1, -1))


def neighbours():
    sizes = (lax.axis_size("gx"), lax.axis_size("gy"))
    me = (lax.axis_index("gx"), lax.axis_index("gy"))

    def there(d):
        return (me[0] + d[0], me[1] + d[1])

    def exists(d):
        ok = None
        for size, at, step in zip(sizes, me, d):
            if step == 0:
                continue
            test = (at + 1 < size) if step > 0 else (at > 0)
            ok = test if ok is None else jnp.logical_and(ok, test)
        return ok

    return there, exists


def exchange(sends, lands, send_sem, recv_sem, before=None):
    there, exists = neighbours()
    barrier = pltpu.get_barrier_semaphore()
    for d in DIRS:
        @pl.when(exists(d))
        def _(d=d):
            pl.semaphore_signal(barrier, inc=1, device_id=there(d), device_id_type=MESH)
    near = [exists(d).astype(jnp.int32) for d in DIRS[:4]]
    pl.semaphore_wait(barrier, (near[0] + near[1] + 1) * (near[2] + near[3] + 1) - 1)

    def copy(k, d):
        return pltpu.make_async_remote_copy(
            src_ref=sends[k], dst_ref=lands[k], send_sem=send_sem.at[k], recv_sem=recv_sem.at[k],
            device_id=there(d), device_id_type=MESH)

    for k, d in enumerate(DIRS):
        @pl.when(exists(d))
        def _(k=k, d=d):
            copy(k, d).start()

    def finish():
        for k, d in enumerate(DIRS):
            @pl.when(exists((-d[0], -d[1])))
            def _(k=k, d=d):
                copy(k, d).wait_recv()
        for k, d in enumerate(DIRS):
            @pl.when(exists(d))
            def _(k=k, d=d):
                copy(k, d).wait_send()

    return finish


def gram_kernel(c_ref, permit_ref, shift_ref, codes_ref, counts_ref, gram_ref, cs, ts, own_sem, send_sem, recv_sem):
    bx, by, coupling, order = c_ref.shape
    slots = codes_ref.shape[0]
    wide = by + 2
    there, exists = neighbours()
    row = {1: bx - 1, -1: 0}
    col = {1: by - 1, -1: 0}
    land_row = {1: 0, -1: bx + 1}
    land_col = {1: 0, -1: by + 1}
    gx_dirs, gy_dirs, corners = DIRS[:2], DIRS[2:4], DIRS[4:]
    own = [pltpu.make_async_copy(c_ref.at[x], cs.at[pl.ds((x + 1) * wide + 1, by)], own_sem.at[x]) for x in range(bx)]
    for copy in own:
        copy.start()
    barrier = pltpu.get_barrier_semaphore()
    for d in DIRS:
        @pl.when(exists(d))
        def _(d=d):
            pl.semaphore_signal(barrier, inc=1, device_id=there(d), device_id_type=MESH)
    near = [exists(d).astype(jnp.int32) for d in DIRS[:4]]
    pl.semaphore_wait(barrier, (near[0] + near[1] + 1) * (near[2] + near[3] + 1) - 1)

    def remote(source, target, k, d):
        return pltpu.make_async_remote_copy(
            src_ref=source, dst_ref=cs.at[target], send_sem=send_sem.at[k], recv_sem=recv_sem.at[k],
            device_id=there(d), device_id_type=MESH)

    def gy_copy(j, x):
        d = gy_dirs[j]
        return remote(c_ref.at[x, col[d[1]]], (x + 1) * wide + land_col[d[1]], 4 + j * bx + x, d)

    def corner_copy(j):
        d = corners[j]
        return remote(c_ref.at[row[d[0]], col[d[1]]], land_row[d[0]] * wide + land_col[d[1]], j, d)

    def gx_copy(j, y):
        d = gx_dirs[j]
        return remote(c_ref.at[row[d[0]], y], land_row[d[0]] * wide + y + 1, 4 + 2 * bx + 2 * y + j, d)

    for j, d in enumerate(corners):
        @pl.when(exists(d))
        def _(j=j):
            corner_copy(j).start()
    for j, d in enumerate(gx_dirs):
        @pl.when(exists(d))
        def _(j=j):
            for y in range(by):
                gx_copy(j, y).start()
    for j, d in enumerate(gy_dirs):
        @pl.when(exists(d))
        def _(j=j):
            for x in range(bx):
                gy_copy(j, x).start()

    zero = jnp.zeros((coupling, order), cs.dtype)
    for j, d in enumerate(corners):
        @pl.when(jnp.logical_not(exists((-d[0], -d[1]))))
        def _(d=d):
            cs[land_row[d[0]] * wide + land_col[d[1]]] = zero
    for j, d in enumerate(gx_dirs):
        @pl.when(jnp.logical_not(exists((-d[0], -d[1]))))
        def _(d=d):
            @pl.loop(0, by)
            def _(y):
                cs[land_row[d[0]] * wide + y + 1] = zero
    for j, d in enumerate(gy_dirs):
        @pl.when(jnp.logical_not(exists((-d[0], -d[1]))))
        def _(d=d):
            for x in range(bx):
                cs[(x + 1) * wide + land_col[d[1]]] = zero

    def turn(n):
        ts[n] = cs[n].T

    def terms(x, y, pairs):
        p = permit_ref[x, pl.ds(y, 1), :]
        acc = None
        for ax, ay in pairs:
            n = (x + ax) * wide + y + ay
            times = jnp.int32(0)
            for s in range(slots):
                hit = (codes_ref[s, x, y] == ax * 3 + ay) & (s < counts_ref[x, y])
                times = times + hit.astype(jnp.int32)
            scaled = (ts[n].astype(jnp.float32) * p).astype(jnp.bfloat16)
            term = times.astype(jnp.float32) * jnp.dot(scaled, cs[n], preferred_element_type=jnp.float32)
            acc = term if acc is None else acc + term
        return acc

    inside = {x: [ax for ax in range(3) if 0 <= x + ax - 1 < bx] for x in range(bx)}
    outside = {x: [ax for ax in range(3) if not 0 <= x + ax - 1 < bx] for x in range(bx)}
    for copy in own:
        copy.wait()
    for x in range(bx):
        @pl.loop(0, by)
        def _(y):
            turn((x + 1) * wide + y + 1)
    for x in range(bx):
        @pl.loop(1, by - 1)
        def _(y):
            gram_ref[x, y] = terms(x, y, [(ax, ay) for ax in inside[x] for ay in range(3)])
    for j, d in enumerate(gy_dirs):
        @pl.when(exists((-d[0], -d[1])))
        def _(j=j):
            for x in range(bx):
                gy_copy(j, x).wait_recv()
    for x in range(bx):
        turn((x + 1) * wide)
        turn((x + 1) * wide + by + 1)
    for x in range(bx):
        @pl.loop(0, 2)
        def _(e):
            y = e * (by - 1)
            gram_ref[x, y] = terms(x, y, [(ax, ay) for ax in inside[x] for ay in range(3)])

    same = lax.broadcasted_iota(jnp.int32, (order, order), 0) == lax.broadcasted_iota(jnp.int32, (order, order), 1)

    def finished(x, y, acc):
        gram_ref[x, y] = 0.5 * (acc + acc.T) + jnp.where(same, shift_ref[x, pl.ds(y, 1), :], 0.0)

    for x in range(1, bx - 1):
        @pl.loop(0, by)
        def _(y):
            finished(x, y, gram_ref[x, y])
    for j, d in enumerate(corners):
        @pl.when(exists((-d[0], -d[1])))
        def _(j=j):
            corner_copy(j).wait_recv()
    for r in (0, bx + 1):
        turn(r * wide)
        turn(r * wide + by + 1)

    def arrive(y):
        for j, d in enumerate(gx_dirs):
            @pl.when(exists((-d[0], -d[1])))
            def _(j=j):
                gx_copy(j, y).wait_recv()
        turn(y + 1)
        turn((bx + 1) * wide + y + 1)

    def last(y):
        for x in sorted({0, bx - 1}):
            finished(x, y, gram_ref[x, y] + terms(x, y, [(ax, ay) for ax in outside[x] for ay in range(3)]))

    arrive(0)

    @pl.loop(1, by)
    def _(y):
        arrive(y)
        last(y - 1)

    last(by - 1)
    for j, d in enumerate(corners):
        @pl.when(exists(d))
        def _(j=j):
            corner_copy(j).wait_send()
    for j, d in enumerate(gx_dirs):
        @pl.when(exists(d))
        def _(j=j):
            for y in range(by):
                gx_copy(j, y).wait_send()
    for j, d in enumerate(gy_dirs):
        @pl.when(exists(d))
        def _(j=j):
            for x in range(bx):
                gy_copy(j, x).wait_send()


def factor_kernel(gram_ref, codes_ref, counts_ref, weights_ref, v_ref, fac_ref, loc_ref, px_ref, py_ref, pc_ref, gs, ss):
    bx, by, order = gram_ref.shape[:3]
    slots = codes_ref.shape[0]
    blocks = bx * by
    wide = by + 2
    nx, ny = lax.axis_size("gx"), lax.axis_size("gy")
    gx, gy = lax.axis_index("gx"), lax.axis_index("gy")

    @pl.loop(0, (bx + 2) * wide)
    def _(n):
        ss[n] = jnp.zeros(ss.shape[1:], ss.dtype)

    for i in range(blocks):
        gs[i] = gram_ref[i // by, i % by]

    def slot_at(x, y, s):
        code = codes_ref[s, x, y]
        ax, ay = code // 3, code % 3
        whole_x, whole_y = gx * bx + x + ax - 1, gy * by + y + ay - 1
        ok = (s < counts_ref[x, y]) & (whole_x >= 0) & (whole_x < nx * bx) & (whole_y >= 0) & (whole_y < ny * by)
        return jnp.where(ok, (x + ax) * wide + y + ay, (x + 1) * wide + y + 1), ok

    lanes = lax.broadcasted_iota(jnp.int32, (order, order), 1)
    per = order // BASE
    seg = lax.broadcasted_iota(jnp.int32, (BASE, order), 1) // BASE
    place = lax.broadcasted_iota(jnp.int32, (BASE, order), 1) % BASE
    row = lax.broadcasted_iota(jnp.int32, (BASE, order), 0)
    for stage in range(per):
        low = stage * BASE
        high = low + BASE
        packs = []
        for g in range(blocks // per):
            pack = None
            for q in range(per):
                piece = gs[g * per + q, low:high, :]
                shift = (q * BASE - low) % order
                piece = pltpu.roll(piece, shift, axis=1) if shift else piece
                pack = piece if pack is None else jnp.where(seg == q, piece, pack)
            packs.append(pack)
        done = [[] for _ in packs]
        scale = [[] for _ in packs]
        for k in range(0, BASE, 2):
            top = k // 8 * 8
            at, nxt = k - top, k + 1 - top
            for g, m in enumerate(packs):
                f = jnp.take_along_axis(m, seg[top:] * BASE + k, axis=1)
                f_next = jnp.take_along_axis(m, seg[top:] * BASE + (k + 1), axis=1)
                d = f[at:at + 1]
                inv_d = 1.0 / d
                scale[g].append(lax.rsqrt(d))
                f = jnp.where(row[top:] > k, f, 0.0)
                f_next = f_next - f * (f_next[at:at + 1] * inv_d)
                d_next = f_next[nxt:nxt + 1]
                scale[g].append(lax.rsqrt(d_next))
                m = m - f * ((m[at:at + 1] + jnp.where(place[:1] == k, 1.0, 0.0)) * inv_d)
                f_next = jnp.where(row[top:] > k + 1, f_next, 0.0)
                r_next = m[nxt:nxt + 1] + jnp.where(place[:1] == k + 1, 1.0, 0.0)
                m = m - f_next * (r_next * (1.0 / d_next))
                if k % 8 == 6:
                    done[g].append(m[:8])
                    m = m[8:]
                packs[g] = m
        for g in range(len(packs)):
            m = jnp.concatenate(done[g], axis=0)
            unit = jnp.where(row > place, m, jnp.where(row == place, 1.0, 0.0))
            inv = unit * jnp.concatenate(scale[g], axis=0)
            wide_inv = jnp.concatenate([jnp.where(seg == q, inv, 0.0) for q in range(per)], axis=0)
            panel = []
            for q in range(per):
                here = gs[g * per + q, low:high, :]
                panel.append(jnp.where(seg == stage, jnp.where(row == place, 1.0, 0.0), here))
            panel = jnp.concatenate(panel, axis=0)
            whole = jnp.dot(wide_inv, panel, precision=lax.Precision.HIGHEST, preferred_element_type=jnp.float32)
            for q in range(per):
                at = g * per + q
                part = whole[q * BASE:(q + 1) * BASE]
                gs[at, low:high, :] = jnp.where(seg <= stage, part, 0.0)
                if high < order:
                    h = part.astype(jnp.bfloat16)
                    rest = part - h.astype(jnp.float32)
                    m = rest.astype(jnp.bfloat16)
                    l = (rest - m.astype(jnp.float32)).astype(jnp.bfloat16)
                    update = lax.dot_general(
                        jnp.concatenate([h, h, m, h, l, m], axis=0), jnp.concatenate([h, m, h, l, h, m], axis=0),
                        (((0,), (0,)), ((), ())), preferred_element_type=jnp.float32)
                    below = gs[at, high:, :]
                    below = jnp.where(lanes[high:] // BASE == stage, 0.0, below)
                    gs[at, high:, :] = below - update[high:]

    @pl.loop(0, blocks)
    def _(i):
        x, y = i // by, i % by
        factor = gs[i].astype(jnp.bfloat16)
        fac_ref[x, y] = factor
        image = lax.dot_general(factor, v_ref[x, y], (((0,), (0,)), ((), ())), preferred_element_type=jnp.float32)
        for s in range(slots):
            n, ok = slot_at(x, y, s)
            w = jnp.where(ok, weights_ref[s, x, y], 0.0)
            ss[n] = ss[n] + w * image

    for x in range(bx):
        for y in range(by):
            loc_ref[x, y] = ss[(x + 1) * wide + y + 1]
        py_ref[1, x] = ss[(x + 1) * wide].astype(jnp.bfloat16)
        py_ref[0, x] = ss[(x + 1) * wide + by + 1].astype(jnp.bfloat16)
    for y in range(by):
        px_ref[1, y] = ss[y + 1].astype(jnp.bfloat16)
        px_ref[0, y] = ss[(bx + 1) * wide + y + 1].astype(jnp.bfloat16)
    pc_ref[0] = ss[(bx + 1) * wide + by + 1].astype(jnp.bfloat16)
    pc_ref[1] = ss[(bx + 1) * wide].astype(jnp.bfloat16)
    pc_ref[2] = ss[by + 1].astype(jnp.bfloat16)
    pc_ref[3] = ss[0].astype(jnp.bfloat16)


def sum_kernel(loc_ref, px_ref, py_ref, pc_ref, out_ref, rx, ry, rc, send_sem, recv_sem):
    bx, by = loc_ref.shape[0], loc_ref.shape[1]
    _, exists = neighbours()
    sends = [px_ref.at[0], px_ref.at[1], py_ref.at[0], py_ref.at[1]] + [pc_ref.at[k] for k in range(4)]
    lands = [rx.at[0], rx.at[1], ry.at[0], ry.at[1]] + [rc.at[k] for k in range(4)]
    for k, d in enumerate(DIRS):
        @pl.when(jnp.logical_not(exists((-d[0], -d[1]))))
        def _(k=k):
            lands[k][...] = jnp.zeros(lands[k].shape, lands[k].dtype)
    exchange(sends, lands, send_sem, recv_sem)()
    corner = {(0, 0): 0, (0, by - 1): 1, (bx - 1, 0): 2, (bx - 1, by - 1): 3}
    for x in range(bx):
        for y in range(by):
            total = loc_ref[x, y]
            for at, edge, k in ((x, 0, 0), (x, bx - 1, 1)):
                if at == edge:
                    total = total + rx[k, y].astype(jnp.float32)
            for at, edge, k in ((y, 0, 0), (y, by - 1, 1)):
                if at == edge:
                    total = total + ry[k, x].astype(jnp.float32)
            for place, k in (((0, 0), 0), ((0, by - 1), 1), ((bx - 1, 0), 2), ((bx - 1, by - 1), 3)):
                if (x, y) == place:
                    total = total + rc[k].astype(jnp.float32)
            out_ref[x, y] = total.astype(out_ref.dtype)


def local(coeffs, permit, shift_diag, codes, counts, weights, vectors):
    bx, by, coupling, order = coeffs.shape
    nv = vectors.shape[3]
    bf16, f32 = jnp.bfloat16, jnp.float32
    anyspace = pl.BlockSpec(memory_space=pl.ANY)
    vmem = pl.BlockSpec(memory_space=pltpu.VMEM)
    smem = pl.BlockSpec(memory_space=pltpu.SMEM)
    codes, weights = jnp.transpose(codes, (2, 0, 1)), jnp.transpose(weights, (2, 0, 1))
    padded = (bx + 2) * (by + 2)
    copies = 4 + 2 * bx + 2 * by
    gram = pl.pallas_call(
        gram_kernel,
        out_shape=jax.ShapeDtypeStruct((bx, by, order, order), f32),
        in_specs=[anyspace, vmem, vmem, smem, smem],
        out_specs=vmem,
        scratch_shapes=[
            pltpu.VMEM((padded, coupling, order), bf16),
            pltpu.VMEM((padded, order, coupling), bf16),
            pltpu.SemaphoreType.DMA((bx,)),
            pltpu.SemaphoreType.DMA((copies,)), pltpu.SemaphoreType.DMA((copies,)),
        ],
        compiler_params=pltpu.CompilerParams(collective_id=0, has_side_effects=True),
        name="gram",
    )(coeffs, permit, shift_diag, codes, counts)
    fac, loc, px, py, pc = pl.pallas_call(
        factor_kernel,
        out_shape=(
            jax.ShapeDtypeStruct((bx, by, order, order), bf16),
            jax.ShapeDtypeStruct((bx, by, order, nv), f32),
            jax.ShapeDtypeStruct((2, by, order, nv), bf16),
            jax.ShapeDtypeStruct((2, bx, order, nv), bf16),
            jax.ShapeDtypeStruct((4, order, nv), bf16),
        ),
        in_specs=[vmem, smem, smem, smem, vmem],
        out_specs=(vmem,) * 5,
        scratch_shapes=[
            pltpu.VMEM((bx * by, order, order), f32),
            pltpu.VMEM((padded, order, nv), f32),
        ],
        name="factor",
    )(gram, codes, counts, weights, vectors)
    applied = pl.pallas_call(
        sum_kernel,
        out_shape=jax.ShapeDtypeStruct((bx, by, order, nv), bf16),
        in_specs=[vmem, anyspace, anyspace, anyspace],
        out_specs=vmem,
        scratch_shapes=[
            pltpu.VMEM((2, by, order, nv), bf16),
            pltpu.VMEM((2, bx, order, nv), bf16),
            pltpu.VMEM((4, order, nv), bf16),
            pltpu.SemaphoreType.DMA((8,)), pltpu.SemaphoreType.DMA((8,)),
        ],
        compiler_params=pltpu.CompilerParams(collective_id=1, has_side_effects=True),
        name="sums",
    )(loc, px, py, pc)
    return fac, applied


def solution(mesh):
    placed = (
        P("gx", "gy", None, None),
        P("gx", "gy", None),
        P("gx", "gy", None),
        P("gx", "gy", None),
        P("gx", "gy"),
        P("gx", "gy", None),
        P("gx", "gy", None, None),
    )
    return jax.shard_map(
        local,
        mesh=mesh,
        in_specs=placed,
        out_specs=(P("gx", "gy", None, None), P("gx", "gy", None, None)),
        check_vma=False,
    )
```

```python
import functools

import jax
import jax.numpy as jnp
from jax import lax
from jax.experimental import pallas as pl
from jax.experimental.pallas import tpu as pltpu
from jax.sharding import PartitionSpec as P

MESH = pl.DeviceIdType.MESH
BASE = 32
DIRS = ((1, 0), (-1, 0), (0, 1), (0, -1), (1, 1), (1, -1), (-1, 1), (-1, -1))


def neighbours():
    sizes = (lax.axis_size("gx"), lax.axis_size("gy"))
    me = (lax.axis_index("gx"), lax.axis_index("gy"))

    def there(d):
        return (me[0] + d[0], me[1] + d[1])

    def exists(d):
        ok = None
        for size, at, step in zip(sizes, me, d):
            if step == 0:
                continue
            test = (at + 1 < size) if step > 0 else (at > 0)
            ok = test if ok is None else jnp.logical_and(ok, test)
        return ok

    return there, exists


def gram_kernel(c_ref, permit_ref, shift_ref, codes_ref, counts_ref, gram_ref, cs, ts, own_sem, send_sem, recv_sem):
    bx, by, coupling, order = c_ref.shape
    slots = codes_ref.shape[0]
    wide = by + 2
    there, exists = neighbours()
    row = {1: bx - 1, -1: 0}
    col = {1: by - 1, -1: 0}
    land_row = {1: 0, -1: bx + 1}
    land_col = {1: 0, -1: by + 1}
    gx_dirs, gy_dirs, corners = DIRS[:2], DIRS[2:4], DIRS[4:]
    own = [pltpu.make_async_copy(c_ref.at[x], cs.at[pl.ds((x + 1) * wide + 1, by)], own_sem.at[x]) for x in range(bx)]
    for copy in own:
        copy.start()
    barrier = pltpu.get_barrier_semaphore()
    for d in DIRS:
        @pl.when(exists(d))
        def _(d=d):
            pl.semaphore_signal(barrier, inc=1, device_id=there(d), device_id_type=MESH)
    near = [exists(d).astype(jnp.int32) for d in DIRS[:4]]
    pl.semaphore_wait(barrier, (near[0] + near[1] + 1) * (near[2] + near[3] + 1) - 1)

    def remote(source, target, k, d):
        return pltpu.make_async_remote_copy(
            src_ref=source, dst_ref=cs.at[target], send_sem=send_sem.at[k], recv_sem=recv_sem.at[k],
            device_id=there(d), device_id_type=MESH)

    def gy_copy(j, x):
        d = gy_dirs[j]
        return remote(c_ref.at[x, col[d[1]]], (x + 1) * wide + land_col[d[1]], 4 + j * bx + x, d)

    def corner_copy(j):
        d = corners[j]
        return remote(c_ref.at[row[d[0]], col[d[1]]], land_row[d[0]] * wide + land_col[d[1]], j, d)

    def gx_copy(j, y):
        d = gx_dirs[j]
        return remote(c_ref.at[row[d[0]], y], land_row[d[0]] * wide + y + 1, 4 + 2 * bx + 2 * y + j, d)

    for j, d in enumerate(corners):
        @pl.when(exists(d))
        def _(j=j):
            corner_copy(j).start()
    for j, d in enumerate(gx_dirs):
        @pl.when(exists(d))
        def _(j=j):
            for y in range(by):
                gx_copy(j, y).start()
    for j, d in enumerate(gy_dirs):
        @pl.when(exists(d))
        def _(j=j):
            for x in range(bx):
                gy_copy(j, x).start()

    zero = jnp.zeros((coupling, order), cs.dtype)
    for j, d in enumerate(corners):
        @pl.when(jnp.logical_not(exists((-d[0], -d[1]))))
        def _(d=d):
            cs[land_row[d[0]] * wide + land_col[d[1]]] = zero
    for j, d in enumerate(gx_dirs):
        @pl.when(jnp.logical_not(exists((-d[0], -d[1]))))
        def _(d=d):
            @pl.loop(0, by)
            def _(y):
                cs[land_row[d[0]] * wide + y + 1] = zero
    for j, d in enumerate(gy_dirs):
        @pl.when(jnp.logical_not(exists((-d[0], -d[1]))))
        def _(d=d):
            for x in range(bx):
                cs[(x + 1) * wide + land_col[d[1]]] = zero

    def turn(n):
        ts[n] = cs[n].T

    def terms(x, y, pairs):
        p = permit_ref[x, pl.ds(y, 1), :]
        acc = None
        for ax, ay in pairs:
            n = (x + ax) * wide + y + ay
            times = jnp.int32(0)
            for s in range(slots):
                hit = (codes_ref[s, x, y] == ax * 3 + ay) & (s < counts_ref[x, y])
                times = times + hit.astype(jnp.int32)
            scaled = (ts[n].astype(jnp.float32) * p).astype(jnp.bfloat16)
            term = times.astype(jnp.float32) * jnp.dot(scaled, cs[n], preferred_element_type=jnp.float32)
            acc = term if acc is None else acc + term
        return acc

    inside = {x: [ax for ax in range(3) if 0 <= x + ax - 1 < bx] for x in range(bx)}
    outside = {x: [ax for ax in range(3) if not 0 <= x + ax - 1 < bx] for x in range(bx)}
    for copy in own:
        copy.wait()
    for x in range(bx):
        @pl.loop(0, by)
        def _(y):
            turn((x + 1) * wide + y + 1)
    for x in range(bx):
        @pl.loop(1, by - 1)
        def _(y):
            gram_ref[x, y] = terms(x, y, [(ax, ay) for ax in inside[x] for ay in range(3)])
    for j, d in enumerate(gy_dirs):
        @pl.when(exists((-d[0], -d[1])))
        def _(j=j):
            for x in range(bx):
                gy_copy(j, x).wait_recv()
    for x in range(bx):
        turn((x + 1) * wide)
        turn((x + 1) * wide + by + 1)
    for x in range(bx):
        @pl.loop(0, 2)
        def _(e):
            y = e * (by - 1)
            gram_ref[x, y] = terms(x, y, [(ax, ay) for ax in inside[x] for ay in range(3)])

    same = lax.broadcasted_iota(jnp.int32, (order, order), 0) == lax.broadcasted_iota(jnp.int32, (order, order), 1)

    def finished(x, y, acc):
        gram_ref[x, y] = 0.5 * (acc + acc.T) + jnp.where(same, shift_ref[x, pl.ds(y, 1), :], 0.0)

    for x in range(1, bx - 1):
        @pl.loop(0, by)
        def _(y):
            finished(x, y, gram_ref[x, y])
    for j, d in enumerate(corners):
        @pl.when(exists((-d[0], -d[1])))
        def _(j=j):
            corner_copy(j).wait_recv()
    for r in (0, bx + 1):
        turn(r * wide)
        turn(r * wide + by + 1)

    def arrive(y):
        for j, d in enumerate(gx_dirs):
            @pl.when(exists((-d[0], -d[1])))
            def _(j=j):
                gx_copy(j, y).wait_recv()
        turn(y + 1)
        turn((bx + 1) * wide + y + 1)

    def last(y):
        for x in sorted({0, bx - 1}):
            finished(x, y, gram_ref[x, y] + terms(x, y, [(ax, ay) for ax in outside[x] for ay in range(3)]))

    arrive(0)

    @pl.loop(1, by)
    def _(y):
        arrive(y)
        last(y - 1)

    last(by - 1)
    for j, d in enumerate(corners):
        @pl.when(exists(d))
        def _(j=j):
            corner_copy(j).wait_send()
    for j, d in enumerate(gx_dirs):
        @pl.when(exists(d))
        def _(j=j):
            for y in range(by):
                gx_copy(j, y).wait_send()
    for j, d in enumerate(gy_dirs):
        @pl.when(exists(d))
        def _(j=j):
            for x in range(bx):
                gy_copy(j, x).wait_send()


def factor_kernel(gram_ref, fac_ref, gs):
    bx, by, order = gram_ref.shape[:3]
    blocks = bx * by
    for i in range(blocks):
        gs[i] = gram_ref[i // by, i % by]

    lanes = lax.broadcasted_iota(jnp.int32, (order, order), 1)
    per = order // BASE
    seg = lax.broadcasted_iota(jnp.int32, (BASE, order), 1) // BASE
    place = lax.broadcasted_iota(jnp.int32, (BASE, order), 1) % BASE
    row = lax.broadcasted_iota(jnp.int32, (BASE, order), 0)
    for stage in range(per):
        low = stage * BASE
        high = low + BASE
        packs = []
        for g in range(blocks // per):
            pack = None
            for q in range(per):
                piece = gs[g * per + q, low:high, :]
                shift = (q * BASE - low) % order
                piece = pltpu.roll(piece, shift, axis=1) if shift else piece
                pack = piece if pack is None else jnp.where(seg == q, piece, pack)
            packs.append(pack)
        done = [[] for _ in packs]
        scale = [[] for _ in packs]
        for k in range(0, BASE, 2):
            top = k // 8 * 8
            at, nxt = k - top, k + 1 - top
            for g, m in enumerate(packs):
                f = jnp.take_along_axis(m, seg[top:] * BASE + k, axis=1)
                f_next = jnp.take_along_axis(m, seg[top:] * BASE + (k + 1), axis=1)
                d = f[at:at + 1]
                inv_d = 1.0 / d
                scale[g].append(lax.rsqrt(d))
                f = jnp.where(row[top:] > k, f, 0.0)
                f_next = f_next - f * (f_next[at:at + 1] * inv_d)
                d_next = f_next[nxt:nxt + 1]
                scale[g].append(lax.rsqrt(d_next))
                m = m - f * ((m[at:at + 1] + jnp.where(place[:1] == k, 1.0, 0.0)) * inv_d)
                f_next = jnp.where(row[top:] > k + 1, f_next, 0.0)
                r_next = m[nxt:nxt + 1] + jnp.where(place[:1] == k + 1, 1.0, 0.0)
                m = m - f_next * (r_next * (1.0 / d_next))
                if k % 8 == 6:
                    done[g].append(m[:8])
                    m = m[8:]
                packs[g] = m
        for g in range(len(packs)):
            m = jnp.concatenate(done[g], axis=0)
            unit = jnp.where(row > place, m, jnp.where(row == place, 1.0, 0.0))
            inv = unit * jnp.concatenate(scale[g], axis=0)
            wide_inv = jnp.concatenate([jnp.where(seg == q, inv, 0.0) for q in range(per)], axis=0)
            panel = []
            for q in range(per):
                here = gs[g * per + q, low:high, :]
                panel.append(jnp.where(seg == stage, jnp.where(row == place, 1.0, 0.0), here))
            panel = jnp.concatenate(panel, axis=0)
            whole = jnp.dot(wide_inv, panel, precision=lax.Precision.HIGHEST, preferred_element_type=jnp.float32)
            for q in range(per):
                at = g * per + q
                part = whole[q * BASE:(q + 1) * BASE]
                gs[at, low:high, :] = jnp.where(seg <= stage, part, 0.0)
                if high < order:
                    h = part.astype(jnp.bfloat16)
                    rest = part - h.astype(jnp.float32)
                    m = rest.astype(jnp.bfloat16)
                    l = (rest - m.astype(jnp.float32)).astype(jnp.bfloat16)
                    update = lax.dot_general(
                        jnp.concatenate([h, h, m, h, l, m], axis=0), jnp.concatenate([h, m, h, l, h, m], axis=0),
                        (((0,), (0,)), ((), ())), preferred_element_type=jnp.float32)
                    below = gs[at, high:, :]
                    below = jnp.where(lanes[high:] // BASE == stage, 0.0, below)
                    gs[at, high:, :] = below - update[high:]

    @pl.loop(0, blocks)
    def _(i):
        fac_ref[i // by, i % by] = gs[i].astype(fac_ref.dtype)


def sum_kernel(fac_ref, v_ref, codes_ref, counts_ref, weights_ref, out_ref, img, loc, px, py, pc, rx, ry, rc, wt,
               send_sem, recv_sem):
    bx, by = fac_ref.shape[:2]
    slots = codes_ref.shape[0]
    there, exists = neighbours()
    sends = [px.at[0], px.at[1], py.at[0], py.at[1]] + [pc.at[k] for k in range(4)]
    lands = [rx.at[0], rx.at[1], ry.at[0], ry.at[1]] + [rc.at[k] for k in range(4)]
    barrier = pltpu.get_barrier_semaphore()
    for d in DIRS:
        @pl.when(exists(d))
        def _(d=d):
            pl.semaphore_signal(barrier, inc=1, device_id=there(d), device_id_type=MESH)
    for k, d in enumerate(DIRS):
        @pl.when(jnp.logical_not(exists((-d[0], -d[1]))))
        def _(k=k):
            lands[k][...] = jnp.zeros(lands[k].shape, lands[k].dtype)

    @pl.loop(0, by)
    def _(y):
        for x in range(bx):
            for offset in range(9):
                w = jnp.float32(0.0)
                for s in range(slots):
                    hit = (codes_ref[s, x, y] == offset) & (s < counts_ref[x, y])
                    w = w + jnp.where(hit, weights_ref[s, x, y], 0.0)
                wt[offset, x * by + y] = w
            img[x, y] = lax.dot_general(fac_ref[x, y], v_ref[x, y], (((0,), (0,)), ((), ())),
                                        preferred_element_type=jnp.float32)

    def target(tx, ty):
        total = None
        for x in range(bx):
            for y in range(by):
                ax, ay = tx - x, ty - y
                if 0 <= ax < 3 and 0 <= ay < 3:
                    term = wt[ax * 3 + ay, x * by + y] * img[x, y]
                    total = term if total is None else total + term
        return total

    for y in range(by):
        px[0, y] = target(bx + 1, y + 1).astype(px.dtype)
        px[1, y] = target(0, y + 1).astype(px.dtype)
    for k, d in enumerate(DIRS[4:]):
        pc[k] = target(bx + 1 if d[0] > 0 else 0, by + 1 if d[1] > 0 else 0).astype(pc.dtype)
    for x in range(bx):
        py[0, x] = target(x + 1, by + 1).astype(py.dtype)
        py[1, x] = target(x + 1, 0).astype(py.dtype)
    near = [exists(d).astype(jnp.int32) for d in DIRS[:4]]
    pl.semaphore_wait(barrier, (near[0] + near[1] + 1) * (near[2] + near[3] + 1) - 1)

    def copy(k, d):
        return pltpu.make_async_remote_copy(
            src_ref=sends[k], dst_ref=lands[k], send_sem=send_sem.at[k], recv_sem=recv_sem.at[k],
            device_id=there(d), device_id_type=MESH)

    order_of = (4, 5, 6, 7, 0, 1, 2, 3)
    for k in order_of:
        @pl.when(exists(DIRS[k]))
        def _(k=k):
            copy(k, DIRS[k]).start()
    for x in range(bx):
        for y in range(by):
            loc[x, y] = target(x + 1, y + 1)
    for k in order_of:
        @pl.when(exists((-DIRS[k][0], -DIRS[k][1])))
        def _(k=k):
            copy(k, DIRS[k]).wait_recv()
    for x in range(bx):
        for y in range(by):
            total = loc[x, y]
            for k, edge in ((0, 0), (1, bx - 1)):
                if x == edge:
                    total = total + rx[k, y].astype(jnp.float32)
            for k, edge in ((0, 0), (1, by - 1)):
                if y == edge:
                    total = total + ry[k, x].astype(jnp.float32)
            for k, place in enumerate(((0, 0), (0, by - 1), (bx - 1, 0), (bx - 1, by - 1))):
                if (x, y) == place:
                    total = total + rc[k].astype(jnp.float32)
            out_ref[x, y] = total.astype(out_ref.dtype)
    for k in order_of:
        @pl.when(exists(DIRS[k]))
        def _(k=k):
            copy(k, DIRS[k]).wait_send()


def local(coeffs, permit, shift_diag, codes, counts, weights, vectors):
    bx, by, coupling, order = coeffs.shape
    nv = vectors.shape[3]
    bf16, f32 = jnp.bfloat16, jnp.float32
    anyspace = pl.BlockSpec(memory_space=pl.ANY)
    vmem = pl.BlockSpec(memory_space=pltpu.VMEM)
    smem = pl.BlockSpec(memory_space=pltpu.SMEM)
    codes, weights = jnp.transpose(codes, (2, 0, 1)), jnp.transpose(weights, (2, 0, 1))
    padded = (bx + 2) * (by + 2)
    copies = 4 + 2 * bx + 2 * by
    gram = pl.pallas_call(
        gram_kernel,
        out_shape=jax.ShapeDtypeStruct((bx, by, order, order), f32),
        in_specs=[anyspace, vmem, vmem, smem, smem],
        out_specs=vmem,
        scratch_shapes=[
            pltpu.VMEM((padded, coupling, order), bf16),
            pltpu.VMEM((padded, order, coupling), bf16),
            pltpu.SemaphoreType.DMA((bx,)),
            pltpu.SemaphoreType.DMA((copies,)), pltpu.SemaphoreType.DMA((copies,)),
        ],
        compiler_params=pltpu.CompilerParams(collective_id=0, has_side_effects=True),
        name="gram",
    )(coeffs, permit, shift_diag, codes, counts)
    fac = pl.pallas_call(
        factor_kernel,
        out_shape=jax.ShapeDtypeStruct((bx, by, order, order), bf16),
        in_specs=[vmem],
        out_specs=vmem,
        scratch_shapes=[pltpu.VMEM((bx * by, order, order), f32)],
        name="factor",
    )(gram)
    edges = [
        pltpu.VMEM((2, by, order, nv), bf16),
        pltpu.VMEM((2, bx, order, nv), bf16),
        pltpu.VMEM((4, order, nv), bf16),
    ]
    applied = pl.pallas_call(
        sum_kernel,
        out_shape=jax.ShapeDtypeStruct((bx, by, order, nv), bf16),
        in_specs=[vmem, vmem, smem, smem, smem],
        out_specs=vmem,
        scratch_shapes=[
            pltpu.VMEM((bx, by, order, nv), f32),
            pltpu.VMEM((bx, by, order, nv), f32),
            *edges, *edges,
            pltpu.SMEM((9, bx * by), f32),
            pltpu.SemaphoreType.DMA((8,)), pltpu.SemaphoreType.DMA((8,)),
        ],
        compiler_params=pltpu.CompilerParams(collective_id=1, has_side_effects=True),
        name="sums",
    )(fac, vectors, codes, counts, weights)
    return fac, applied


def solution(mesh):
    placed = (
        P("gx", "gy", None, None),
        P("gx", "gy", None),
        P("gx", "gy", None),
        P("gx", "gy", None),
        P("gx", "gy"),
        P("gx", "gy", None),
        P("gx", "gy", None, None),
    )
    return jax.shard_map(
        local,
        mesh=mesh,
        in_specs=placed,
        out_specs=(P("gx", "gy", None, None), P("gx", "gy", None, None)),
        check_vma=False,
    )
```

```python
import functools

import jax
import jax.numpy as jnp
from jax import lax
from jax.experimental import pallas as pl
from jax.experimental.pallas import tpu as pltpu
from jax.sharding import PartitionSpec as P

MESH = pl.DeviceIdType.MESH
BASE = 32
DIRS = ((1, 0), (-1, 0), (0, 1), (0, -1), (1, 1), (1, -1), (-1, 1), (-1, -1))


def neighbours():
    sizes = (lax.axis_size("gx"), lax.axis_size("gy"))
    me = (lax.axis_index("gx"), lax.axis_index("gy"))

    def there(d):
        return (me[0] + d[0], me[1] + d[1])

    def exists(d):
        ok = None
        for size, at, step in zip(sizes, me, d):
            if step == 0:
                continue
            test = (at + 1 < size) if step > 0 else (at > 0)
            ok = test if ok is None else jnp.logical_and(ok, test)
        return ok

    return there, exists


def gram_kernel(c_ref, permit_ref, shift_ref, codes_ref, counts_ref, weights_ref, gram_ref, wt, cs, ts, own_sem, send_sem, recv_sem):
    bx, by, coupling, order = c_ref.shape
    slots = codes_ref.shape[0]
    wide = by + 2
    there, exists = neighbours()
    row = {1: bx - 1, -1: 0}
    col = {1: by - 1, -1: 0}
    land_row = {1: 0, -1: bx + 1}
    land_col = {1: 0, -1: by + 1}
    gx_dirs, gy_dirs, corners = DIRS[:2], DIRS[2:4], DIRS[4:]
    own = [pltpu.make_async_copy(c_ref.at[x], cs.at[pl.ds((x + 1) * wide + 1, by)], own_sem.at[x]) for x in range(bx)]
    for copy in own:
        copy.start()
    barrier = pltpu.get_barrier_semaphore()
    for d in DIRS:
        @pl.when(exists(d))
        def _(d=d):
            pl.semaphore_signal(barrier, inc=1, device_id=there(d), device_id_type=MESH)
    near = [exists(d).astype(jnp.int32) for d in DIRS[:4]]
    pl.semaphore_wait(barrier, (near[0] + near[1] + 1) * (near[2] + near[3] + 1) - 1)

    def remote(source, target, k, d):
        return pltpu.make_async_remote_copy(
            src_ref=source, dst_ref=cs.at[target], send_sem=send_sem.at[k], recv_sem=recv_sem.at[k],
            device_id=there(d), device_id_type=MESH)

    def gy_copy(j, x):
        d = gy_dirs[j]
        return remote(c_ref.at[x, col[d[1]]], (x + 1) * wide + land_col[d[1]], 4 + j * bx + x, d)

    def corner_copy(j):
        d = corners[j]
        return remote(c_ref.at[row[d[0]], col[d[1]]], land_row[d[0]] * wide + land_col[d[1]], j, d)

    def gx_copy(j, y):
        d = gx_dirs[j]
        return remote(c_ref.at[row[d[0]], y], land_row[d[0]] * wide + y + 1, 4 + 2 * bx + 2 * y + j, d)

    for j, d in enumerate(corners):
        @pl.when(exists(d))
        def _(j=j):
            corner_copy(j).start()
    for j, d in enumerate(gx_dirs):
        @pl.when(exists(d))
        def _(j=j):
            for y in range(by):
                gx_copy(j, y).start()
    for j, d in enumerate(gy_dirs):
        @pl.when(exists(d))
        def _(j=j):
            for x in range(bx):
                gy_copy(j, x).start()

    zero = jnp.zeros((coupling, order), cs.dtype)
    for j, d in enumerate(corners):
        @pl.when(jnp.logical_not(exists((-d[0], -d[1]))))
        def _(d=d):
            cs[land_row[d[0]] * wide + land_col[d[1]]] = zero
    for j, d in enumerate(gx_dirs):
        @pl.when(jnp.logical_not(exists((-d[0], -d[1]))))
        def _(d=d):
            @pl.loop(0, by)
            def _(y):
                cs[land_row[d[0]] * wide + y + 1] = zero
    for j, d in enumerate(gy_dirs):
        @pl.when(jnp.logical_not(exists((-d[0], -d[1]))))
        def _(d=d):
            for x in range(bx):
                cs[(x + 1) * wide + land_col[d[1]]] = zero

    def turn(n):
        ts[n] = cs[n].T

    def terms(x, y, pairs):
        p = permit_ref[x, pl.ds(y, 1), :]
        acc = None
        for ax, ay in pairs:
            n = (x + ax) * wide + y + ay
            times = jnp.int32(0)
            for s in range(slots):
                hit = (codes_ref[s, x, y] == ax * 3 + ay) & (s < counts_ref[x, y])
                times = times + hit.astype(jnp.int32)
            scaled = (ts[n].astype(jnp.float32) * p).astype(jnp.bfloat16)
            term = times.astype(jnp.float32) * jnp.dot(scaled, cs[n], preferred_element_type=jnp.float32)
            acc = term if acc is None else acc + term
        return acc

    inside = {x: [ax for ax in range(3) if 0 <= x + ax - 1 < bx] for x in range(bx)}
    outside = {x: [ax for ax in range(3) if not 0 <= x + ax - 1 < bx] for x in range(bx)}

    @pl.loop(0, by)
    def _(y):
        for x in range(bx):
            for offset in range(9):
                w = jnp.float32(0.0)
                for s in range(slots):
                    hit = (codes_ref[s, x, y] == offset) & (s < counts_ref[x, y])
                    w = w + jnp.where(hit, weights_ref[s, x, y], 0.0)
                wt[offset, x * by + y] = w

    for copy in own:
        copy.wait()
    for x in range(bx):
        @pl.loop(0, by)
        def _(y):
            turn((x + 1) * wide + y + 1)
    for x in range(bx):
        @pl.loop(1, by - 1)
        def _(y):
            gram_ref[x, y] = terms(x, y, [(ax, ay) for ax in inside[x] for ay in range(3)])
    for j, d in enumerate(gy_dirs):
        @pl.when(exists((-d[0], -d[1])))
        def _(j=j):
            for x in range(bx):
                gy_copy(j, x).wait_recv()
    for x in range(bx):
        turn((x + 1) * wide)
        turn((x + 1) * wide + by + 1)
    for x in range(bx):
        @pl.loop(0, 2)
        def _(e):
            y = e * (by - 1)
            gram_ref[x, y] = terms(x, y, [(ax, ay) for ax in inside[x] for ay in range(3)])

    same = lax.broadcasted_iota(jnp.int32, (order, order), 0) == lax.broadcasted_iota(jnp.int32, (order, order), 1)

    def finished(x, y, acc):
        gram_ref[x, y] = 0.5 * (acc + acc.T) + jnp.where(same, shift_ref[x, pl.ds(y, 1), :], 0.0)

    for x in range(1, bx - 1):
        @pl.loop(0, by)
        def _(y):
            finished(x, y, gram_ref[x, y])
    for j, d in enumerate(corners):
        @pl.when(exists((-d[0], -d[1])))
        def _(j=j):
            corner_copy(j).wait_recv()
    for r in (0, bx + 1):
        turn(r * wide)
        turn(r * wide + by + 1)

    def arrive(y):
        for j, d in enumerate(gx_dirs):
            @pl.when(exists((-d[0], -d[1])))
            def _(j=j):
                gx_copy(j, y).wait_recv()
        turn(y + 1)
        turn((bx + 1) * wide + y + 1)

    def last(y):
        for x in sorted({0, bx - 1}):
            finished(x, y, gram_ref[x, y] + terms(x, y, [(ax, ay) for ax in outside[x] for ay in range(3)]))

    arrive(0)

    @pl.loop(1, by)
    def _(y):
        arrive(y)
        last(y - 1)

    last(by - 1)
    for j, d in enumerate(corners):
        @pl.when(exists(d))
        def _(j=j):
            corner_copy(j).wait_send()
    for j, d in enumerate(gx_dirs):
        @pl.when(exists(d))
        def _(j=j):
            for y in range(by):
                gx_copy(j, y).wait_send()
    for j, d in enumerate(gy_dirs):
        @pl.when(exists(d))
        def _(j=j):
            for x in range(bx):
                gy_copy(j, x).wait_send()


def factor_kernel(gram_ref, fac_ref, gs):
    bx, by, order = gram_ref.shape[:3]
    blocks = bx * by
    for i in range(blocks):
        gs[i] = gram_ref[i // by, i % by]

    lanes = lax.broadcasted_iota(jnp.int32, (order, order), 1)
    per = order // BASE
    seg = lax.broadcasted_iota(jnp.int32, (BASE, order), 1) // BASE
    place = lax.broadcasted_iota(jnp.int32, (BASE, order), 1) % BASE
    row = lax.broadcasted_iota(jnp.int32, (BASE, order), 0)
    for stage in range(per):
        low = stage * BASE
        high = low + BASE
        packs = []
        for g in range(blocks // per):
            pack = None
            for q in range(per):
                piece = gs[g * per + q, low:high, :]
                shift = (q * BASE - low) % order
                piece = pltpu.roll(piece, shift, axis=1) if shift else piece
                pack = piece if pack is None else jnp.where(seg == q, piece, pack)
            packs.append(pack)
        done = [[] for _ in packs]
        scale = [[] for _ in packs]
        for k in range(0, BASE, 2):
            top = k // 8 * 8
            at, nxt = k - top, k + 1 - top
            for g, m in enumerate(packs):
                f = jnp.take_along_axis(m, seg[top:] * BASE + k, axis=1)
                f_next = jnp.take_along_axis(m, seg[top:] * BASE + (k + 1), axis=1)
                d = f[at:at + 1]
                inv_d = 1.0 / d
                scale[g].append(lax.rsqrt(d))
                f = jnp.where(row[top:] > k, f, 0.0)
                f_next = f_next - f * (f_next[at:at + 1] * inv_d)
                d_next = f_next[nxt:nxt + 1]
                scale[g].append(lax.rsqrt(d_next))
                m = m - f * ((m[at:at + 1] + jnp.where(place[:1] == k, 1.0, 0.0)) * inv_d)
                f_next = jnp.where(row[top:] > k + 1, f_next, 0.0)
                r_next = m[nxt:nxt + 1] + jnp.where(place[:1] == k + 1, 1.0, 0.0)
                m = m - f_next * (r_next * (1.0 / d_next))
                if k % 8 == 6:
                    done[g].append(m[:8])
                    m = m[8:]
                packs[g] = m
        for g in range(len(packs)):
            m = jnp.concatenate(done[g], axis=0)
            unit = jnp.where(row > place, m, jnp.where(row == place, 1.0, 0.0))
            inv = unit * jnp.concatenate(scale[g], axis=0)
            wide_inv = jnp.concatenate([jnp.where(seg == q, inv, 0.0) for q in range(per)], axis=0)
            panel = []
            for q in range(per):
                here = gs[g * per + q, low:high, :]
                panel.append(jnp.where(seg == stage, jnp.where(row == place, 1.0, 0.0), here))
            panel = jnp.concatenate(panel, axis=0)
            whole = jnp.dot(wide_inv, panel, precision=lax.Precision.HIGHEST, preferred_element_type=jnp.float32)
            for q in range(per):
                at = g * per + q
                part = whole[q * BASE:(q + 1) * BASE]
                gs[at, low:high, :] = jnp.where(seg <= stage, part, 0.0)
                if high < order:
                    h = part.astype(jnp.bfloat16)
                    rest = part - h.astype(jnp.float32)
                    m = rest.astype(jnp.bfloat16)
                    l = (rest - m.astype(jnp.float32)).astype(jnp.bfloat16)
                    update = lax.dot_general(
                        jnp.concatenate([h, h, m, h, l, m], axis=0), jnp.concatenate([h, m, h, l, h, m], axis=0),
                        (((0,), (0,)), ((), ())), preferred_element_type=jnp.float32)
                    below = gs[at, high:, :]
                    below = jnp.where(lanes[high:] // BASE == stage, 0.0, below)
                    gs[at, high:, :] = below - update[high:]

    @pl.loop(0, blocks)
    def _(i):
        fac_ref[i // by, i % by] = gs[i].astype(fac_ref.dtype)


def sum_kernel(fac_ref, v_ref, wt, out_ref, img, loc, px, py, pc, rx, ry, rc, send_sem, recv_sem):
    bx, by = fac_ref.shape[:2]
    there, exists = neighbours()
    sends = [px.at[0], px.at[1], py.at[0], py.at[1]] + [pc.at[k] for k in range(4)]
    lands = [rx.at[0], rx.at[1], ry.at[0], ry.at[1]] + [rc.at[k] for k in range(4)]
    barrier = pltpu.get_barrier_semaphore()
    for d in DIRS:
        @pl.when(exists(d))
        def _(d=d):
            pl.semaphore_signal(barrier, inc=1, device_id=there(d), device_id_type=MESH)
    for k, d in enumerate(DIRS):
        @pl.when(jnp.logical_not(exists((-d[0], -d[1]))))
        def _(k=k):
            lands[k][...] = jnp.zeros(lands[k].shape, lands[k].dtype)

    @pl.loop(0, by)
    def _(y):
        for x in range(bx):
            img[x, y] = lax.dot_general(fac_ref[x, y], v_ref[x, y], (((0,), (0,)), ((), ())),
                                        preferred_element_type=jnp.float32)

    def target(tx, ty):
        total = None
        for x in range(bx):
            for y in range(by):
                ax, ay = tx - x, ty - y
                if 0 <= ax < 3 and 0 <= ay < 3:
                    term = wt[ax * 3 + ay, x * by + y] * img[x, y]
                    total = term if total is None else total + term
        return total

    for y in range(by):
        px[0, y] = target(bx + 1, y + 1).astype(px.dtype)
        px[1, y] = target(0, y + 1).astype(px.dtype)
    for k, d in enumerate(DIRS[4:]):
        pc[k] = target(bx + 1 if d[0] > 0 else 0, by + 1 if d[1] > 0 else 0).astype(pc.dtype)
    for x in range(bx):
        py[0, x] = target(x + 1, by + 1).astype(py.dtype)
        py[1, x] = target(x + 1, 0).astype(py.dtype)
    near = [exists(d).astype(jnp.int32) for d in DIRS[:4]]
    pl.semaphore_wait(barrier, (near[0] + near[1] + 1) * (near[2] + near[3] + 1) - 1)

    def copy(k, d):
        return pltpu.make_async_remote_copy(
            src_ref=sends[k], dst_ref=lands[k], send_sem=send_sem.at[k], recv_sem=recv_sem.at[k],
            device_id=there(d), device_id_type=MESH)

    order_of = (4, 5, 6, 7, 0, 1, 2, 3)
    for k in order_of:
        @pl.when(exists(DIRS[k]))
        def _(k=k):
            copy(k, DIRS[k]).start()
    for x in range(bx):
        for y in range(by):
            loc[x, y] = target(x + 1, y + 1)
    for k in order_of:
        @pl.when(exists((-DIRS[k][0], -DIRS[k][1])))
        def _(k=k):
            copy(k, DIRS[k]).wait_recv()
    for x in range(bx):
        for y in range(by):
            total = loc[x, y]
            for k, edge in ((0, 0), (1, bx - 1)):
                if x == edge:
                    total = total + rx[k, y].astype(jnp.float32)
            for k, edge in ((0, 0), (1, by - 1)):
                if y == edge:
                    total = total + ry[k, x].astype(jnp.float32)
            for k, place in enumerate(((0, 0), (0, by - 1), (bx - 1, 0), (bx - 1, by - 1))):
                if (x, y) == place:
                    total = total + rc[k].astype(jnp.float32)
            out_ref[x, y] = total.astype(out_ref.dtype)
    for k in order_of:
        @pl.when(exists(DIRS[k]))
        def _(k=k):
            copy(k, DIRS[k]).wait_send()


def local(coeffs, permit, shift_diag, codes, counts, weights, vectors):
    bx, by, coupling, order = coeffs.shape
    nv = vectors.shape[3]
    bf16, f32 = jnp.bfloat16, jnp.float32
    anyspace = pl.BlockSpec(memory_space=pl.ANY)
    vmem = pl.BlockSpec(memory_space=pltpu.VMEM)
    smem = pl.BlockSpec(memory_space=pltpu.SMEM)
    codes, weights = jnp.transpose(codes, (2, 0, 1)), jnp.transpose(weights, (2, 0, 1))
    padded = (bx + 2) * (by + 2)
    copies = 4 + 2 * bx + 2 * by
    gram, sums = pl.pallas_call(
        gram_kernel,
        out_shape=(jax.ShapeDtypeStruct((bx, by, order, order), f32), jax.ShapeDtypeStruct((9, bx * by), f32)),
        in_specs=[anyspace, vmem, vmem, smem, smem, smem],
        out_specs=(vmem, smem),
        scratch_shapes=[
            pltpu.VMEM((padded, coupling, order), bf16),
            pltpu.VMEM((padded, order, coupling), bf16),
            pltpu.SemaphoreType.DMA((bx,)),
            pltpu.SemaphoreType.DMA((copies,)), pltpu.SemaphoreType.DMA((copies,)),
        ],
        compiler_params=pltpu.CompilerParams(collective_id=0, has_side_effects=True),
        name="gram",
    )(coeffs, permit, shift_diag, codes, counts, weights)
    fac = pl.pallas_call(
        factor_kernel,
        out_shape=jax.ShapeDtypeStruct((bx, by, order, order), bf16),
        in_specs=[vmem],
        out_specs=vmem,
        scratch_shapes=[pltpu.VMEM((bx * by, order, order), f32)],
        name="factor",
    )(gram)
    edges = [
        pltpu.VMEM((2, by, order, nv), bf16),
        pltpu.VMEM((2, bx, order, nv), bf16),
        pltpu.VMEM((4, order, nv), bf16),
    ]
    applied = pl.pallas_call(
        sum_kernel,
        out_shape=jax.ShapeDtypeStruct((bx, by, order, nv), bf16),
        in_specs=[vmem, vmem, smem],
        out_specs=vmem,
        scratch_shapes=[
            pltpu.VMEM((bx, by, order, nv), f32),
            pltpu.VMEM((bx, by, order, nv), f32),
            *edges, *edges,
            pltpu.SemaphoreType.DMA((8,)), pltpu.SemaphoreType.DMA((8,)),
        ],
        compiler_params=pltpu.CompilerParams(collective_id=1, has_side_effects=True),
        name="sums",
    )(fac, vectors, sums)
    return fac, applied


def solution(mesh):
    placed = (
        P("gx", "gy", None, None),
        P("gx", "gy", None),
        P("gx", "gy", None),
        P("gx", "gy", None),
        P("gx", "gy"),
        P("gx", "gy", None),
        P("gx", "gy", None, None),
    )
    return jax.shard_map(
        local,
        mesh=mesh,
        in_specs=placed,
        out_specs=(P("gx", "gy", None, None), P("gx", "gy", None, None)),
        check_vma=False,
    )
```
